32 devices in a mesh: ctx: 8 (over z, y), tp: 4 (over x, core).
Axes of the slice: x: 2, y: 2, z: 4, core: 2. Of those that a mesh axis runs over, the one named last changes fastest.
Arguments:
- grad_out: bfloat16 [1024, 8192], P('ctx', 'tp'), may hold values from -40 to 40
- query_in: bfloat16 [1024, 8192], P('ctx', 'tp'), may hold values from -6 to 6
- key_in: bfloat16 [1024, 8192], P('ctx', 'tp'), may hold values from -6 to 6
- value_in: bfloat16 [1024, 8192], P('ctx', 'tp'), may hold values from -6 to 6
- residue: float32 [8192, 16], P('tp'), may hold values from -4 to 4
- log_rate: float32 [8192, 16], P('tp'), may hold values from -14 to -3, as said below
Outputs:
- grad_query: bfloat16 [1024, 8192], P('ctx', 'tp')
- grad_key: bfloat16 [1024, 8192], P('ctx', 'tp')
- grad_value: bfloat16 [1024, 8192], P('ctx', 'tp')
- residue_grad: float32 [8192, 16], P('tp')
- rate_grad: float32 [8192, 16], P('tp')
The draws below stay inside these ranges and needn't reach their ends.
Inputs may be any that keep to these rules, and one draw needn't show every extreme that they name: `log_rate`: exp of an entry is the decay per position of one filter mode.
All inputs are finite; a program needn't handle non-finite values.
Results may differ from the reference program's by a relative error of at most 0.001.
Values sent between devices are 32-bit elements; how exact they have to be, the bound alone decides.
A program may use at most 64 MiB of HBM per device.

```python
import math
import jax
import jax.numpy as jnp
from jax import lax

D = 8192
MODES = 16
CLIP_NORM = 512
SEQ = 1024


def draw_log_rate(key, part):
    pick_key, slow_key, fast_key = jax.random.split(jax.random.fold_in(key, 7), 3)
    top_rate = math.log(math.log(10.0) / SEQ)
    slow_rates = jax.random.uniform(slow_key, (D, MODES), jnp.float32, top_rate - math.log(10.0), top_rate)
    fast_rates = jax.random.uniform(fast_key, (D, MODES), jnp.float32, top_rate, -3.0)
    slow_share = 0.5
    chosen = jax.random.uniform(pick_key, (D, MODES), jnp.float32) < slow_share
    return jnp.where(chosen, slow_rates, fast_rates).astype(jnp.float32)


def draw_grad_out(key, part):
    level_key, base_key = jax.random.split(jax.random.fold_in(key, 13), 2)
    channel = jnp.arange(D, dtype=jnp.float32)
    levels = jax.random.uniform(level_key, (D,), jnp.float32, 0.0, 1.0)
    base_draw = jax.random.truncated_normal(base_key, -4.0, 4.0, (SEQ, D), jnp.float32)
    channel_scale = jnp.exp(levels * math.log(10.0) + channel / (D - 1) * math.log(3.0)) / 3.0
    return (base_draw * channel_scale[None, :]).astype(jnp.bfloat16)


def shard_levels(own_key, shape, pieces, low, largest):
    gain = 1.0
    for axis_at, parts in pieces:
        draws = jax.random.uniform(jax.random.fold_in(jax.random.fold_in(own_key, 6), axis_at), (parts,), jnp.float32, low / len(pieces), largest / len(pieces))
        gain = gain * jnp.repeat(jnp.exp(draws), shape[axis_at] // parts).reshape((-1,) + (1,) * (len(shape) - 1 - axis_at))
    return gain


def centred(stream_key, extent, spread, limit, cuts=(), held_as=jnp.bfloat16):
    level = shard_levels(stream_key, extent, cuts, -0.22, 0.18) if cuts else 1.0
    drawn = jax.random.normal(stream_key, extent, jnp.float32) * spread * level
    return jnp.minimum(jnp.maximum(drawn, -limit), limit).astype(held_as)


def setup_inputs(seed: int = 0) -> dict:
    key_of = jax.random.split(jax.random.key(seed), 7)
    grad_out = draw_grad_out(jax.random.fold_in(key_of[6], 71), 0)
    query_in = centred(key_of[1], (SEQ, D), 1.0, 6.0, ((0, 8), (1, 4)))
    key_in = centred(key_of[2], (SEQ, D), 1.0, 6.0, ((0, 8), (1, 4)))
    value_in = centred(key_of[3], (SEQ, D), 1.0, 6.0, ((0, 8), (1, 4)))
    residue = centred(key_of[4], (D, MODES), 0.25, 4.0, ((0, 4),), jnp.float32)
    log_rate = draw_log_rate(jax.random.fold_in(key_of[6], 71), 0)
    return {"grad_out": grad_out, "query_in": query_in, "key_in": key_in, "value_in": value_in, "residue": residue, "log_rate": log_rate}


def reference(grad_out, query_in, key_in, value_in, residue, log_rate):
    decay_rate = jnp.exp(log_rate)
    decay_step = jnp.exp(-decay_rate)
    mode_weight = residue * jnp.sqrt(2.0 * decay_rate)
    product = key_in.astype(jnp.float32) * value_in.astype(jnp.float32)
    gated_grad = grad_out.astype(jnp.float32) * query_in.astype(jnp.float32)
    zero_state = jnp.zeros(residue.shape, jnp.float32)

    def forward_step(carried, inputs_row):
        states, lagged, weight_sum, lag_total = carried
        product_row, gated_row = inputs_row
        lagged = decay_step * (lagged + states)
        states = decay_step * states + product_row[:, None]
        weight_sum = weight_sum + gated_row[:, None] * states
        lag_total = lag_total + gated_row[:, None] * lagged
        return ((states, lagged, weight_sum, lag_total), lax.optimization_barrier(jnp.sum(mode_weight * states, axis=1)))
    start_value = (zero_state, zero_state, zero_state, zero_state)
    finals, filtered = lax.scan(forward_step, start_value, (product, gated_grad))
    raw_weight = finals[2]
    lag_total = finals[3]

    def backward_step(adjoint, gated_row):
        adjoint = decay_step * adjoint + gated_row[:, None]
        return (adjoint, lax.optimization_barrier(jnp.sum(mode_weight * adjoint, axis=1)))
    _, back_filtered = lax.scan(backward_step, zero_state, gated_grad, reverse=True)
    grad_query = (grad_out.astype(jnp.float32) * filtered).astype(jnp.bfloat16)
    grad_key = (back_filtered * value_in.astype(jnp.float32)).astype(jnp.bfloat16)
    grad_value = (back_filtered * key_in.astype(jnp.float32)).astype(jnp.bfloat16)
    raw_residue = jnp.sqrt(2.0 * decay_rate) * raw_weight
    raw_rate = mode_weight * (0.5 * raw_weight - decay_rate * lag_total)
    squares = jnp.sum(raw_residue * raw_residue) + jnp.sum(raw_rate * raw_rate)
    grad_scale = jnp.minimum(1.0, CLIP_NORM / jnp.sqrt(squares + 1e-06))
    return (grad_query, grad_key, grad_value, raw_residue * grad_scale, raw_rate * grad_scale)
```

```python
import functools

import jax
import jax.numpy as jnp
from jax import lax
from jax.experimental import pallas as pl
from jax.experimental.pallas import tpu as pltpu
from jax.sharding import PartitionSpec as P

CLIP_NORM = 512
SUB = 8
LANES = 128
MESH = pl.DeviceIdType.MESH
VMEM_BYTES = 24 * 1024 * 1024


def total_of(terms):
    while len(terms) > 1:
        paired = [x + y for x, y in zip(terms[::2], terms[1::2])]
        terms = paired + ([terms[-1]] if len(terms) % 2 else [])
    return terms[0]


def fused_kernel(
    n, ntp, modes, groups,
    go_ref, q_ref, k_ref, v_ref, lr_ref, res_ref,
    gq_ref, gk_ref, gv_ref, dres_ref, drate_ref,
    p_s, g_s, ends_s, pre_s, loc_s, turn_s, lag_s, hold_s, table, fr_s, br_s,
    ea_s, mate, pt_s, held, ca_s, back_s, raw_s, parts, red, gath, sums, squares,
    pa_send, pa_recv, ex_send, ex_recv, bk_send, bk_recv,
    rs_send, rs_recv, ag_send, ag_recv, sq_send, sq_recv,
):
    me = lax.axis_index("ctx")
    pair = me // 2
    odd = lax.rem(me, 2)
    pairs = n // 2
    total = n * ntp
    here = me * ntp + lax.axis_index("tp")
    rows, chans = go_ref.shape
    span = rows // SUB
    width = chans // groups
    half = width // 2
    per_group = width // LANES
    per_half = half // LANES
    pieces = 2 * modes // SUB
    own = raw_s.shape[1] // n
    zero = jnp.zeros((SUB, LANES), jnp.float32)
    folds = modes // SUB

    def place(q):
        other = lax.rem(here + q, total)
        return {"ctx": other // ntp, "tp": lax.rem(other, ntp)}

    def peer(k):
        return {"ctx": lax.rem(me + k, n)}

    barrier = pltpu.get_barrier_semaphore()

    def greet(q, _):
        pl.semaphore_signal(barrier, inc=1, device_id=place(q), device_id_type=MESH)
        return 0

    lax.fori_loop(1, total, greet, 0)

    def wide(x, m):
        return jnp.broadcast_to(x[m : m + 1], (SUB, LANES))

    def lanes(ch):
        return pl.ds(pl.multiple_of(ch * LANES, LANES), LANES)

    def fold(f):
        return pl.ds(f * SUB, SUB)

    def turned(q, f):
        return pl.ds(f * SUB * SUB + q, SUB, stride=SUB)

    def ends(g):
        def chunk(c, _):
            ch = g * per_group + c
            at = lanes(ch)
            p_s[ch] = k_ref[:, at].astype(jnp.float32) * v_ref[:, at].astype(jnp.float32)
            g_s[ch] = go_ref[:, at].astype(jnp.float32) * q_ref[:, at].astype(jnp.float32)
            rate = jnp.exp(lr_ref[:, at])
            decay = jnp.exp(-rate)
            for first in range(0, modes, 8):
                group = range(first, min(modes, first + 8))
                a = [wide(decay, m) for m in group]
                s = [zero] * len(a)
                t = [zero] * len(a)
                for i in range(span):
                    x = p_s[ch, pl.ds(i, SUB, stride=span), :]
                    y = g_s[ch, pl.ds(span - 1 - i, SUB, stride=span), :]
                    s = [aa * ss + x for aa, ss in zip(a, s)]
                    t = [aa * tt + y for aa, tt in zip(a, t)]
                for slot, m in enumerate(group):
                    ends_s[ch, 0, m * SUB : (m + 1) * SUB] = s[slot]
                    ends_s[ch, 1, m * SUB : (m + 1) * SUB] = t[slot]
            far = jnp.exp(-rate * span)
            side, inner = c // per_half, lanes(lax.rem(c, per_half))
            for f in range(folds):
                step = far[f * SUB : (f + 1) * SUB]
                s = zero
                t = zero
                for q in range(SUB):
                    pre_s[ch, 0, q, fold(f)] = s
                    s = step * s + ends_s[ch, 0, turned(q, f)]
                    pre_s[ch, 1, SUB - 1 - q, fold(f)] = t
                    t = step * t + ends_s[ch, 1, turned(SUB - 1 - q, f)]
                ea_s[g, side, 0, fold(f), inner] = s
                ea_s[g, side, 1, fold(f), inner] = t
            return 0

        lax.fori_loop(0, per_group, chunk, 0)

    def local(g):
        def chunk(c, _):
            ch = g * per_group + c
            rate = jnp.exp(lr_ref[:, lanes(ch)])
            decay = jnp.exp(-rate)
            power = decay
            for k in range(1, span + 1):
                table[k * modes : (k + 1) * modes] = power * float(k)
                power = power * decay
            x = [p_s[ch, pl.ds(b, SUB, stride=span), :] for b in range(span)]
            y = [g_s[ch, pl.ds(b, SUB, stride=span), :] for b in range(span)]
            for m in range(modes):
                da, de = [], []
                for k in range(1, span + 1):
                    coeff = jnp.broadcast_to(table[k * modes + m : k * modes + m + 1], (SUB, LANES))
                    da.append(coeff * y[k - 1])
                    if k < span:
                        de.append(coeff * x[span - 1 - k])
                    if len(da) == 4:
                        da = [total_of(da)]
                    if len(de) == 4:
                        de = [total_of(de)]
                turn_s[0, m * SUB : (m + 1) * SUB] = total_of(da)
                turn_s[1, m * SUB : (m + 1) * SUB] = total_of(de)
            for j in range(span):
                terms = []
                for b in range(span - j):
                    terms.append(y[b + j] * x[b])
                    if len(terms) == 4:
                        terms = [total_of(terms)]
                lag_s[j * SUB : (j + 1) * SUB] = total_of(terms)
            for f in range(span // SUB):
                hold_s[f * SUB : (f + 1) * SUB] = total_of([lag_s[turned(q, f)] for q in range(SUB)])
            far = jnp.exp(-rate * span)
            for f in range(folds):
                a = decay[f * SUB : (f + 1) * SUB]
                step = far[f * SUB : (f + 1) * SUB]
                v = zero
                d = zero
                for j in reversed(range(span)):
                    d = a * d + v
                    v = a * v + jnp.broadcast_to(hold_s[j : j + 1], (SUB, LANES))
                z = a * step * float(span)
                raw = zero
                lag = zero
                ahead = zero
                behind = zero
                for q in range(SUB):
                    before = pre_s[ch, 0, q, fold(f)]
                    after = pre_s[ch, 1, q, fold(f)]
                    u = turn_s[0, turned(q, f)] + z * after
                    w = a * turn_s[1, turned(q, f)]
                    raw = raw + before * ends_s[ch, 1, turned(q, f)]
                    lag = lag + before * u + after * w
                    behind = step * behind + w + z * before
                for q in reversed(range(SUB)):
                    u = turn_s[0, turned(q, f)] + z * pre_s[ch, 1, q, fold(f)]
                    ahead = step * ahead + u
                loc_s[ch, 0, fold(f)] = v + a * raw
                loc_s[ch, 1, fold(f)] = a * d + lag
                loc_s[ch, 2, fold(f)] = ahead
                loc_s[ch, 3, fold(f)] = behind
            return 0

        lax.fori_loop(0, per_group, chunk, 0)

    def couple(g):
        return pltpu.make_async_remote_copy(
            src_ref=ea_s.at[g, 1 - odd],
            dst_ref=mate.at[g],
            send_sem=pa_send.at[g],
            recv_sem=pa_recv.at[g],
            device_id={"ctx": pair * 2 + 1 - odd},
            device_id_type=MESH,
        )

    def exchange(g, k):
        there = lax.rem(pair + k, pairs)
        which = jnp.where(there < pair, 1, 0)
        return pltpu.make_async_remote_copy(
            src_ref=pt_s.at[g, which],
            dst_ref=held.at[g, k - 1],
            send_sem=ex_send.at[g, k - 1],
            recv_sem=ex_recv.at[g, k - 1],
            device_id={"ctx": there * 2 + odd},
            device_id_type=MESH,
        )

    def hand(g):
        return pltpu.make_async_remote_copy(
            src_ref=back_s.at[g],
            dst_ref=ca_s.at[g, odd],
            send_sem=bk_send.at[g],
            recv_sem=bk_recv.at[g],
            device_id={"ctx": pair * 2 + 1 - odd},
            device_id_type=MESH,
        )

    def scatter(g, k):
        there = lax.rem(me + k, n)
        return pltpu.make_async_remote_copy(
            src_ref=raw_s.at[g, pl.ds(there * own, own)],
            dst_ref=parts.at[g, k - 1],
            send_sem=rs_send.at[g, k - 1],
            recv_sem=rs_recv.at[g, k - 1],
            device_id=peer(k),
            device_id_type=MESH,
        )

    def gather(g, k):
        return pltpu.make_async_remote_copy(
            src_ref=red.at[g],
            dst_ref=gath.at[g, me],
            send_sem=ag_send.at[g, k - 1],
            recv_sem=ag_recv.at[g, k - 1],
            device_id=peer(k),
            device_id_type=MESH,
        )

    def norm(q):
        return pltpu.make_async_remote_copy(
            src_ref=squares.at[here],
            dst_ref=squares.at[here],
            send_sem=sq_send.at[q - 1],
            recv_sem=sq_recv.at[q - 1],
            device_id=place(q),
            device_id_type=MESH,
        )

    def rates(g):
        at = pl.ds(pl.multiple_of(g * width + odd * half, LANES), half)
        return jnp.exp(lr_ref[:, at])

    def ordered(g):
        mine, other = ea_s[g, odd], mate[g]
        return jnp.where(odd == 1, other, mine), jnp.where(odd == 1, mine, other)

    def join(g):
        couple(g).wait_recv()
        across = jnp.exp(-rates(g) * rows)
        early, late = ordered(g)
        pt_s[g, 0] = across * early[0] + late[0]
        pt_s[g, 1] = early[1] + across * late[1]
        for k in range(1, pairs):
            exchange(g, k).start()

    def carry(g):
        rate = rates(g)
        back_s[g] = jnp.zeros_like(back_s[g])
        for k in range(1, pairs):
            exchange(g, k).wait_recv()
            origin = lax.rem(pair - k + pairs, pairs)
            which = jnp.where(origin < pair, 0, 1)
            gap = jnp.where(origin < pair, pair - origin, origin - pair) - 1
            power = jnp.exp(-rate * (gap * (2 * rows)).astype(jnp.float32))
            back_s[g, which] += power * held[g, k - 1]
        across = jnp.exp(-rate * rows)
        early, late = ordered(g)
        from_past = back_s[g, 0]
        from_next = back_s[g, 1]
        past = from_past, early[0] + across * from_past
        ahead = late[1] + across * from_next, from_next
        ca_s[g, odd, 0] = jnp.where(odd == 1, past[1], past[0])
        ca_s[g, odd, 1] = jnp.where(odd == 1, ahead[1], ahead[0])
        back_s[g, 0] = jnp.where(odd == 1, past[0], past[1])
        back_s[g, 1] = jnp.where(odd == 1, ahead[0], ahead[1])
        hand(g).start()

    def grads(g):
        def chunk(c, _):
            ch = g * per_group + c
            at = lanes(ch)
            side, inner = c // per_half, lanes(lax.rem(c, per_half))
            rate = jnp.exp(lr_ref[:, at])
            decay = jnp.exp(-rate)
            root = jnp.sqrt(2.0 * rate)
            weight = res_ref[:, at] * root
            past = ca_s[g, side, 0, :, inner]
            ahead = ca_s[g, side, 1, :, inner]
            raw = loc_s[ch, 0] + decay * (past * ea_s[g, side, 1, :, inner])
            through = jnp.exp(-rate * (rows + 1)) * float(rows)
            lag = loc_s[ch, 1] + past * loc_s[ch, 2] + ahead * (loc_s[ch, 3] + through * past)
            both = (root * raw, weight * (0.5 * raw - rate * lag))
            for piece in range(pieces):
                low = piece % (pieces // 2) * SUB
                raw_s[g, c * pieces + piece] = both[piece // (pieces // 2)][low : low + SUB]
            return 0

        lax.fori_loop(0, per_group, chunk, 0)

    def filters(g):
        def chunk(c, _):
            ch = g * per_group + c
            at = lanes(ch)
            side, inner = c // per_half, lanes(lax.rem(c, per_half))
            rate = jnp.exp(lr_ref[:, at])
            decay = jnp.exp(-rate)
            far = jnp.exp(-rate * span)
            for f in range(folds):
                step = far[f * SUB : (f + 1) * SUB]
                past = ca_s[g, side, 0, fold(f), inner]
                ahead = ca_s[g, side, 1, fold(f), inner]
                for q in range(SUB):
                    turn_s[0, turned(q, f)] = pre_s[ch, 0, q, fold(f)] + past
                    turn_s[1, turned(SUB - 1 - q, f)] = pre_s[ch, 1, SUB - 1 - q, fold(f)] + ahead
                    past = step * past
                    ahead = step * ahead
            power = res_ref[:, at] * jnp.sqrt(2.0 * rate)
            for k in range(span + 1):
                table[k * modes : (k + 1) * modes] = power
                power = power * decay
            for f in range(span // SUB):
                hold_s[f * SUB : (f + 1) * SUB] = total_of(
                    [table[pl.ds(f * SUB * modes + m, SUB, stride=modes)] for m in range(modes)]
                )
            h = [jnp.broadcast_to(hold_s[j : j + 1], (SUB, LANES)) for j in range(span)]
            x = [p_s[ch, pl.ds(b, SUB, stride=span), :] for b in range(span)]
            for b in range(span):
                terms = []
                for j in range(b + 1):
                    terms.append(h[j] * x[b - j])
                    if len(terms) == 4:
                        terms = [total_of(terms)]
                lag_s[b * SUB : (b + 1) * SUB] = total_of(terms)
            y = [g_s[ch, pl.ds(b, SUB, stride=span), :] for b in range(span)]
            for b in range(span):
                terms = []
                for j in range(span - b):
                    terms.append(h[j] * y[b + j])
                    if len(terms) == 4:
                        terms = [total_of(terms)]
                lag_s[(span + b) * SUB : (span + b + 1) * SUB] = total_of(terms)
            s = [turn_s[0, m * SUB : (m + 1) * SUB] for m in range(modes)]
            t = [turn_s[1, m * SUB : (m + 1) * SUB] for m in range(modes)]
            for k in range(1, span + 1):
                b = k - 1
                r = span - k
                fore = [lag_s[b * SUB : (b + 1) * SUB]]
                back = [lag_s[(span + r) * SUB : (span + r + 1) * SUB]]
                for m in range(modes):
                    coeff = jnp.broadcast_to(table[k * modes + m : k * modes + m + 1], (SUB, LANES))
                    fore.append(coeff * s[m])
                    back.append(coeff * t[m])
                    if len(fore) == 4:
                        fore = [total_of(fore)]
                        back = [total_of(back)]
                fr_s[pl.ds(b, SUB, stride=span), :] = total_of(fore)
                br_s[pl.ds(r, SUB, stride=span), :] = total_of(back)
            gq_ref[:, at] = (go_ref[:, at].astype(jnp.float32) * fr_s[...]).astype(gq_ref.dtype)
            back = br_s[...]
            gk_ref[:, at] = (back * v_ref[:, at].astype(jnp.float32)).astype(gk_ref.dtype)
            gv_ref[:, at] = (back * k_ref[:, at].astype(jnp.float32)).astype(gv_ref.dtype)
            return 0

        lax.fori_loop(0, per_group, chunk, 0)

    if raw_s.shape[1] > per_group * pieces:
        raw_s[...] = jnp.zeros_like(raw_s)

    def finish(g):
        mine = raw_s[g, pl.ds(me * own, own)]
        for k in range(1, n):
            scatter(g, k).wait_recv()
            mine = mine + parts[g, k - 1]
        red[g] = mine
        for k in range(1, n):
            gather(g, k).start()
        gath[g, me] = mine
        sums[...] += jnp.sum(mine * mine, axis=0)

    def first_stage(g, _):
        ends(g)

        @pl.when(g == 0)
        def _():
            pl.semaphore_wait(barrier, total - 1)

        couple(g).start()

        @pl.when(g > 0)
        def _():
            join(g - 1)

        return 0

    def second_stage(g, _):
        local(g)

        @pl.when(g == min(1, groups - 1))
        def _():
            join(groups - 1)

        return 0

    def third_stage(g, _):
        carry(g)
        return 0

    def fourth_stage(g, _):
        hand(g).wait_recv()
        grads(g)
        for k in range(1, n):
            scatter(g, k).start()
        filters(g)

        @pl.when(g > 0)
        def _():
            finish(g - 1)

        return 0

    sums[...] = zero
    lax.fori_loop(0, groups, first_stage, 0)
    lax.fori_loop(0, groups, second_stage, 0)
    lax.fori_loop(0, groups, third_stage, 0)
    lax.fori_loop(0, groups, fourth_stage, 0)
    finish(groups - 1)
    squares[here] = sums[...]

    def norm_start(q, _):
        norm(q).start()
        return 0

    lax.fori_loop(1, total, norm_start, 0)

    def norm_wait(q, _):
        norm(q).wait()
        return 0

    lax.fori_loop(1, total, norm_wait, 0)
    square = jnp.sum(jnp.sum(squares[...], axis=0), keepdims=True)
    scale = jnp.minimum(1.0, CLIP_NORM / jnp.sqrt(square + 1e-06))
    for g in range(groups):
        for k in range(1, n):
            gather(g, k).wait_recv()
        for c in range(per_group):
            at = pl.ds((g * per_group + c) * LANES, LANES)
            for piece in range(pieces):
                tile = c * pieces + piece
                low = piece % (pieces // 2) * SUB
                ref = dres_ref if piece < pieces // 2 else drate_ref
                ref[low : low + SUB, at] = gath[g, tile // own, tile % own] * scale

    def drain(g, _):
        couple(g).wait_send()
        hand(g).wait_send()
        for k in range(1, pairs):
            exchange(g, k).wait_send()
        for k in range(1, n):
            scatter(g, k).wait_send()
            gather(g, k).wait_send()
        return 0

    lax.fori_loop(0, groups, drain, 0)


def per_device(n, ntp, grad_out, query_in, key_in, value_in, residue, log_rate):
    rows, chans = grad_out.shape
    modes = residue.shape[1]
    span = rows // SUB
    chunks = chans // LANES
    groups = 4 if chunks % 8 == 0 and n <= 32 else 1
    width = chans // groups
    half = width // 2
    own = -(-(width // LANES * 2 * modes // SUB) // n)
    f32 = jnp.float32
    shape = jax.ShapeDtypeStruct
    vmem = pl.BlockSpec(memory_space=pltpu.VMEM)
    buffer = lambda *dims: pltpu.VMEM(dims, f32)
    tile = lambda *lead: pltpu.VMEM((*lead, SUB, LANES), f32)
    flags = lambda *dims: pltpu.SemaphoreType.DMA(dims)
    wide_out = shape((rows, chans), grad_out.dtype)
    tall_out = shape((modes, chans), f32)
    grad_query, grad_key, grad_value, d_res, d_rate = pl.pallas_call(
        functools.partial(fused_kernel, n, ntp, modes, groups),
        out_shape=(wide_out,) * 3 + (tall_out,) * 2,
        in_specs=[vmem] * 6,
        out_specs=(vmem,) * 5,
        scratch_shapes=[
            buffer(chunks, rows, LANES),
            buffer(chunks, rows, LANES),
            buffer(chunks, 2, modes * SUB, LANES),
            buffer(chunks, 2, SUB, modes, LANES),
            buffer(chunks, 4, modes, LANES),
            buffer(2, modes * SUB, LANES),
            buffer(2 * span * SUB, LANES),
            buffer(span, LANES),
            buffer((span + 1) * modes, LANES),
            buffer(rows, LANES),
            buffer(rows, LANES),
            buffer(groups, 2, 2, modes, half),
            buffer(groups, 2, modes, half),
            buffer(groups, 2, modes, half),
            buffer(groups, n // 2 - 1, modes, half),
            buffer(groups, 2, 2, modes, half),
            buffer(groups, 2, modes, half),
            tile(groups, own * n),
            tile(groups, n - 1, own),
            tile(groups, own),
            tile(groups, n, own),
            tile(),
            tile(n * ntp),
            flags(groups), flags(groups),
            flags(groups, n // 2 - 1), flags(groups, n // 2 - 1),
            flags(groups), flags(groups),
            flags(groups, n - 1), flags(groups, n - 1),
            flags(groups, n - 1), flags(groups, n - 1),
            flags(n * ntp - 1), flags(n * ntp - 1),
        ],
        compiler_params=pltpu.CompilerParams(
            collective_id=0, has_side_effects=True, vmem_limit_bytes=VMEM_BYTES
        ),
        name="fused",
    )(grad_out, query_in, key_in, value_in, log_rate.T, residue.T)
    return grad_query, grad_key, grad_value, d_res.T, d_rate.T


def solution(mesh):
    wide = P("ctx", "tp")
    tall = P("tp", None)
    body = functools.partial(per_device, mesh.shape["ctx"], mesh.shape["tp"])
    return jax.shard_map(
        body,
        mesh=mesh,
        in_specs=(wide,) * 4 + (tall,) * 2,
        out_specs=(wide,) * 3 + (tall,) * 2,
        check_vma=False,
    )
```

```python
import functools

import jax
import jax.numpy as jnp
from jax import lax
from jax.experimental import pallas as pl
from jax.experimental.pallas import tpu as pltpu
from jax.sharding import PartitionSpec as P

CLIP_NORM = 512
SUB = 8
LANES = 128
MESH = pl.DeviceIdType.MESH
VMEM_BYTES = 56 * 1024 * 1024
GROUPS = 4
JOIN_AT = 2


def total_of(terms):
    while len(terms) > 1:
        paired = [x + y for x, y in zip(terms[::2], terms[1::2])]
        terms = paired + ([terms[-1]] if len(terms) % 2 else [])
    return terms[0]


def fused_kernel(
    n, ntp, modes, groups,
    go_in, q_in, k_in, v_in, lr_in, res_in,
    for_ref, back_ref, dres_ref, drate_ref,
    go_ref, q_ref, k_ref, v_ref, lr_ref, res_ref,
    p_s, g_s, ends_s, pre_s, loc_s, turn_s, lag_s, hold_s, table, fr_s, br_s,
    ea_s, mate, mate_loc, pt_s, held, ca_s, back_s, raw_s, parts, red, gath, squares,
    in_sem, small_sem, pa_send, pa_recv, pl_send, pl_recv, ex_send, ex_recv, bk_send, bk_recv,
    rs_send, rs_recv, ag_send, ag_recv, fw_send, fw_recv, sq_send, sq_recv,
):
    me = lax.axis_index("ctx")
    col = lax.axis_index("tp")
    pair = me // 2
    odd = lax.rem(me, 2)
    pairs = n // 2
    plane = 2 * ntp
    here = odd * ntp + col
    rows, chans = go_ref.shape
    span = rows // SUB
    width = chans // groups
    half = width // 2
    chunks = chans // LANES
    per_group = width // LANES
    per_half = half // LANES
    pieces = 2 * modes // SUB
    own = red.shape[0]
    zero = jnp.zeros((SUB, LANES), jnp.float32)
    folds = modes // SUB

    def fetch(which, g):
        at = pl.ds(pl.multiple_of(g * width, LANES), width)
        source = (go_in, q_in, k_in, v_in)[which]
        target = (go_ref, q_ref, k_ref, v_ref)[which]
        return pltpu.make_async_copy(source.at[:, at], target.at[:, at], in_sem.at[which, g])

    rate_copy = pltpu.make_async_copy(lr_in, lr_ref, small_sem.at[0])
    residue_copy = pltpu.make_async_copy(res_in, res_ref, small_sem.at[1])
    rate_copy.start()
    for g in range(groups):
        for which in (2, 3, 0, 1):
            fetch(which, g).start()
    residue_copy.start()

    def beside(q):
        other = lax.rem(here + q, plane)
        return {"ctx": pair * 2 + other // ntp, "tp": lax.rem(other, ntp)}

    def along(k):
        return {"ctx": lax.rem(pair + k, pairs) * 2 + odd}

    across_pair = {"ctx": pair * 2 + 1 - odd}
    barrier = pltpu.get_barrier_semaphore()
    for q in range(1, plane):
        pl.semaphore_signal(barrier, inc=1, device_id=beside(q), device_id_type=MESH)
    for k in range(1, pairs):
        pl.semaphore_signal(barrier, inc=1, device_id=along(k), device_id_type=MESH)

    def wide(x, m):
        return jnp.broadcast_to(x[m : m + 1], (SUB, LANES))

    def lanes(ch):
        return pl.ds(pl.multiple_of(ch * LANES, LANES), LANES)

    def fold(f):
        return pl.ds(f * SUB, SUB)

    def turned(q, f):
        return pl.ds(f * SUB * SUB + q, SUB, stride=SUB)

    def copy_to(source, target, send, recv, place):
        return pltpu.make_async_remote_copy(
            src_ref=source, dst_ref=target, send_sem=send, recv_sem=recv, device_id=place, device_id_type=MESH
        )

    def ends(ch):
        g, c = ch // per_group, lax.rem(ch, per_group)
        at = lanes(ch)
        p_s[ch] = k_ref[:, at].astype(jnp.float32) * v_ref[:, at].astype(jnp.float32)
        g_s[ch] = go_ref[:, at].astype(jnp.float32) * q_ref[:, at].astype(jnp.float32)
        rate = jnp.exp(lr_ref[:, at])
        decay = jnp.exp(-rate)
        for first in range(0, modes, 8):
            group = range(first, min(modes, first + 8))
            a = [wide(decay, m) for m in group]
            s = [zero] * len(a)
            t = [zero] * len(a)
            for i in range(span):
                x = p_s[ch, pl.ds(i, SUB, stride=span), :]
                y = g_s[ch, pl.ds(span - 1 - i, SUB, stride=span), :]
                s = [aa * ss + x for aa, ss in zip(a, s)]
                t = [aa * tt + y for aa, tt in zip(a, t)]
            for slot, m in enumerate(group):
                ends_s[ch, 0, m * SUB : (m + 1) * SUB] = s[slot]
                ends_s[ch, 1, m * SUB : (m + 1) * SUB] = t[slot]
        far = jnp.exp(-rate * span)
        side, inner = c // per_half, lanes(lax.rem(c, per_half))
        for f in range(folds):
            step = far[f * SUB : (f + 1) * SUB]
            s = zero
            t = zero
            for q in range(SUB):
                pre_s[ch, 0, q, fold(f)] = s
                s = step * s + ends_s[ch, 0, turned(q, f)]
                pre_s[ch, 1, SUB - 1 - q, fold(f)] = t
                t = step * t + ends_s[ch, 1, turned(SUB - 1 - q, f)]
            ea_s[g, side, 0, fold(f), inner] = s
            ea_s[g, side, 1, fold(f), inner] = t

    def local(ch):
        g, c = ch // per_group, lax.rem(ch, per_group)
        side, inner = c // per_half, lanes(lax.rem(c, per_half))
        rate = jnp.exp(lr_ref[:, lanes(ch)])
        decay = jnp.exp(-rate)
        power = decay
        for k in range(1, span + 1):
            table[k * modes : (k + 1) * modes] = power * float(k)
            power = power * decay
        x = [p_s[ch, pl.ds(b, SUB, stride=span), :] for b in range(span)]
        y = [g_s[ch, pl.ds(b, SUB, stride=span), :] for b in range(span)]
        for m in range(modes):
            da, de = [], []
            for k in range(1, span + 1):
                coeff = jnp.broadcast_to(table[k * modes + m : k * modes + m + 1], (SUB, LANES))
                da.append(coeff * y[k - 1])
                if k < span:
                    de.append(coeff * x[span - 1 - k])
                if len(da) == 4:
                    da = [total_of(da)]
                if len(de) == 4:
                    de = [total_of(de)]
            turn_s[0, m * SUB : (m + 1) * SUB] = total_of(da)
            turn_s[1, m * SUB : (m + 1) * SUB] = total_of(de)
        for j in range(span):
            terms = []
            for b in range(span - j):
                terms.append(y[b + j] * x[b])
                if len(terms) == 4:
                    terms = [total_of(terms)]
            lag_s[j * SUB : (j + 1) * SUB] = total_of(terms)
        for f in range(span // SUB):
            hold_s[f * SUB : (f + 1) * SUB] = total_of([lag_s[turned(q, f)] for q in range(SUB)])
        far = jnp.exp(-rate * span)
        for f in range(folds):
            a = decay[f * SUB : (f + 1) * SUB]
            step = far[f * SUB : (f + 1) * SUB]
            v = zero
            d = zero
            for j in reversed(range(span)):
                d = a * d + v
                v = a * v + jnp.broadcast_to(hold_s[j : j + 1], (SUB, LANES))
            z = a * step * float(span)
            raw = zero
            lag = zero
            ahead = zero
            behind = zero
            for q in range(SUB):
                before = pre_s[ch, 0, q, fold(f)]
                after = pre_s[ch, 1, q, fold(f)]
                u = turn_s[0, turned(q, f)] + z * after
                w = a * turn_s[1, turned(q, f)]
                raw = raw + before * ends_s[ch, 1, turned(q, f)]
                lag = lag + before * u + after * w
                behind = step * behind + w + z * before
            for q in reversed(range(SUB)):
                u = turn_s[0, turned(q, f)] + z * pre_s[ch, 1, q, fold(f)]
                ahead = step * ahead + u
            loc_s[g, side, 0, fold(f), inner] = v + a * raw
            loc_s[g, side, 1, fold(f), inner] = a * d + lag
            loc_s[g, side, 2, fold(f), inner] = ahead
            loc_s[g, side, 3, fold(f), inner] = behind

    def couple(g):
        return copy_to(ea_s.at[g, 1 - odd], mate.at[g], pa_send.at[g], pa_recv.at[g], across_pair)

    def pool(g):
        return copy_to(loc_s.at[g, 1 - odd], mate_loc.at[g], pl_send.at[g], pl_recv.at[g], across_pair)

    def exchange(g, k):
        there = lax.rem(pair + k, pairs)
        which = jnp.where(there < pair, 1, 0)
        return copy_to(
            pt_s.at[g, which], held.at[g, k - 1], ex_send.at[g, k - 1], ex_recv.at[g, k - 1], along(k)
        )

    def hand(g):
        return copy_to(back_s.at[g], ca_s.at[g, odd], bk_send.at[g], bk_recv.at[g], across_pair)

    def scatter(k):
        there = lax.rem(pair + k, pairs)
        return copy_to(
            raw_s.at[pl.ds(there * own, own)], parts.at[k - 1], rs_send.at[k - 1], rs_recv.at[k - 1], along(k)
        )

    def gather(k):
        return copy_to(red, gath.at[odd, pair], ag_send.at[k - 1], ag_recv.at[k - 1], along(k))

    def forward(k):
        slot = lax.rem(pair - k + pairs, pairs)
        return copy_to(gath.at[odd, slot], gath.at[odd, slot], fw_send.at[k], fw_recv.at[k], across_pair)

    def norm(q):
        return copy_to(squares.at[here], squares.at[here], sq_send.at[q - 1], sq_recv.at[q - 1], beside(q))

    def rates(g):
        at = pl.ds(pl.multiple_of(g * width + odd * half, LANES), half)
        return jnp.exp(lr_ref[:, at])

    def ordered(g):
        mine, other = ea_s[g, odd], mate[g]
        return jnp.where(odd == 1, other, mine), jnp.where(odd == 1, mine, other)

    def join(g):
        couple(g).wait_recv()
        across = jnp.exp(-rates(g) * rows)
        early, late = ordered(g)
        pt_s[g, 0] = across * early[0] + late[0]
        pt_s[g, 1] = early[1] + across * late[1]
        for k in range(1, pairs):
            exchange(g, k).start()

    def carry(g):
        rate = rates(g)
        back_s[g] = jnp.zeros_like(back_s[g])
        for k in range(1, pairs):
            exchange(g, k).wait_recv()
            origin = lax.rem(pair - k + pairs, pairs)
            which = jnp.where(origin < pair, 0, 1)
            gap = jnp.where(origin < pair, pair - origin, origin - pair) - 1
            power = jnp.exp(-rate * (gap * (2 * rows)).astype(jnp.float32))
            back_s[g, which] += power * held[g, k - 1]
        across = jnp.exp(-rate * rows)
        early, late = ordered(g)
        from_past = back_s[g, 0]
        from_next = back_s[g, 1]
        past = from_past, early[0] + across * from_past
        ahead = late[1] + across * from_next, from_next
        ca_s[g, odd, 0] = jnp.where(odd == 1, past[1], past[0])
        ca_s[g, odd, 1] = jnp.where(odd == 1, ahead[1], ahead[0])
        back_s[g, 0] = jnp.where(odd == 1, past[0], past[1])
        back_s[g, 1] = jnp.where(odd == 1, ahead[0], ahead[1])
        hand(g).start()

    def grads(i, _):
        g, c = i // per_half, lax.rem(i, per_half)
        inner = lanes(c)
        at = pl.ds(pl.multiple_of(g * width + odd * half + c * LANES, LANES), LANES)
        rate = jnp.exp(lr_ref[:, at])
        decay = jnp.exp(-rate)
        root = jnp.sqrt(2.0 * rate)
        weight = res_ref[:, at] * root
        through = jnp.exp(-rate * (rows + 1)) * float(rows)
        raw, lag = [], []
        for loc, past, ahead, first in (
            (loc_s.at[g, odd], ca_s[g, odd, 0, :, inner], ca_s[g, odd, 1, :, inner], ea_s[g, odd, 1, :, inner]),
            (mate_loc.at[g], back_s[g, 0, :, inner], back_s[g, 1, :, inner], mate[g, 1, :, inner]),
        ):
            raw.append(loc[0, :, inner] + decay * (past * first))
            lag.append(
                loc[1, :, inner] + past * loc[2, :, inner] + ahead * (loc[3, :, inner] + through * past)
            )
        raw_weight = raw[0] + raw[1]
        both = (root * raw_weight, weight * (0.5 * raw_weight - rate * (lag[0] + lag[1])))
        for piece in range(pieces):
            low = piece % (pieces // 2) * SUB
            raw_s[i * pieces + piece] = both[piece // (pieces // 2)][low : low + SUB]
        return 0

    def filters(ch):
        g, c = ch // per_group, lax.rem(ch, per_group)
        side, inner = c // per_half, lanes(lax.rem(c, per_half))
        at = lanes(ch)
        rate = jnp.exp(lr_ref[:, at])
        decay = jnp.exp(-rate)
        far = jnp.exp(-rate * span)
        for f in range(folds):
            step = far[f * SUB : (f + 1) * SUB]
            past = ca_s[g, side, 0, fold(f), inner]
            ahead = ca_s[g, side, 1, fold(f), inner]
            for q in range(SUB):
                turn_s[0, turned(q, f)] = pre_s[ch, 0, q, fold(f)] + past
                turn_s[1, turned(SUB - 1 - q, f)] = pre_s[ch, 1, SUB - 1 - q, fold(f)] + ahead
                past = step * past
                ahead = step * ahead
        power = res_ref[:, at] * jnp.sqrt(2.0 * rate)
        for k in range(span + 1):
            table[k * modes : (k + 1) * modes] = power
            power = power * decay
        for f in range(span // SUB):
            hold_s[f * SUB : (f + 1) * SUB] = total_of(
                [table[pl.ds(f * SUB * modes + m, SUB, stride=modes)] for m in range(modes)]
            )
        h = [jnp.broadcast_to(hold_s[j : j + 1], (SUB, LANES)) for j in range(span)]
        x = [p_s[ch, pl.ds(b, SUB, stride=span), :] for b in range(span)]
        for b in range(span):
            terms = []
            for j in range(b + 1):
                terms.append(h[j] * x[b - j])
                if len(terms) == 4:
                    terms = [total_of(terms)]
            lag_s[b * SUB : (b + 1) * SUB] = total_of(terms)
        y = [g_s[ch, pl.ds(b, SUB, stride=span), :] for b in range(span)]
        for b in range(span):
            terms = []
            for j in range(span - b):
                terms.append(h[j] * y[b + j])
                if len(terms) == 4:
                    terms = [total_of(terms)]
            lag_s[(span + b) * SUB : (span + b + 1) * SUB] = total_of(terms)
        s = [turn_s[0, m * SUB : (m + 1) * SUB] for m in range(modes)]
        t = [turn_s[1, m * SUB : (m + 1) * SUB] for m in range(modes)]
        for k in range(1, span + 1):
            b = k - 1
            r = span - k
            fore = [lag_s[b * SUB : (b + 1) * SUB]]
            back = [lag_s[(span + r) * SUB : (span + r + 1) * SUB]]
            for m in range(modes):
                coeff = jnp.broadcast_to(table[k * modes + m : k * modes + m + 1], (SUB, LANES))
                fore.append(coeff * s[m])
                back.append(coeff * t[m])
                if len(fore) == 4:
                    fore = [total_of(fore)]
                    back = [total_of(back)]
            fr_s[pl.ds(b, SUB, stride=span), :] = total_of(fore)
            br_s[pl.ds(r, SUB, stride=span), :] = total_of(back)
        for_ref[:, at] = fr_s[...]
        back_ref[:, at] = br_s[...]

    if raw_s.shape[0] > chunks // 2 * pieces:
        raw_s[...] = jnp.zeros_like(raw_s)

    def first_stage(ch, _):
        g, c = ch // per_group, lax.rem(ch, per_group)

        @pl.when(c == 0)
        def _():
            for which in range(4):
                fetch(which, g).wait()

        ends(ch)

        @pl.when(ch == per_group - 1)
        def _():
            pl.semaphore_wait(barrier, plane + pairs - 2)

        @pl.when(c == per_group - 1)
        def _():
            couple(g).start()

        return 0

    def second_stage(ch, _):
        for g in range(groups):

            @pl.when(ch == min(JOIN_AT * g, chunks - 1))
            def _(g=g):
                join(g)

        local(ch)

        @pl.when(lax.rem(ch, per_group) == per_group - 1)
        def _():
            pool(ch // per_group).start()

        return 0

    def third_stage(i, _):
        theirs = i // (chunks // 2)
        j = lax.rem(i, chunks // 2)
        g = j // per_half
        side = jnp.where(theirs == 1, 1 - odd, odd)
        opens = lax.rem(j, per_half) == 0

        @pl.when((theirs == 0) & opens)
        def _():
            carry(g)

        @pl.when(i == chunks // 2)
        def _():
            for h in range(groups):
                pool(h).wait_recv()
            lax.fori_loop(0, chunks // 2, grads, 0)
            for k in range(1, pairs):
                scatter(k).start()

        @pl.when((theirs == 1) & opens)
        def _():
            hand(g).wait_recv()

        filters(g * per_group + side * per_half + lax.rem(j, per_half))
        return 0

    rate_copy.wait()
    lax.fori_loop(0, chunks, first_stage, 0)
    lax.fori_loop(0, chunks, second_stage, 0)
    residue_copy.wait()
    lax.fori_loop(0, chunks, third_stage, 0)
    mine = raw_s[pl.ds(pair * own, own)]
    for k in range(1, pairs):
        scatter(k).wait_recv()
        mine = mine + parts[k - 1]
    red[...] = mine
    for k in range(1, pairs):
        gather(k).start()
    gath[odd, pair] = mine
    forward(0).start()
    for k in range(1, pairs):
        gather(k).wait_recv()
        forward(k).start()
    whole = gath[odd]
    squares[here] = jnp.sum(jnp.sum(whole * whole, axis=0), axis=0)
    for q in range(1, plane):
        norm(q).start()
    for q in range(1, plane):
        norm(q).wait()
    square = jnp.sum(jnp.sum(squares[...], axis=0), keepdims=True)
    scale = jnp.minimum(1.0, CLIP_NORM / jnp.sqrt(square + 1e-06))
    for k in range(pairs):
        forward(k).wait_recv()
    for side in range(2):
        for i in range(chunks // 2):
            g, c = i // per_half, i % per_half
            at = pl.ds((g * per_group + side * per_half + c) * LANES, LANES)
            for piece in range(pieces):
                tile = i * pieces + piece
                low = piece % (pieces // 2) * SUB
                ref = dres_ref if piece < pieces // 2 else drate_ref
                ref[low : low + SUB, at] = gath[side, tile // own, tile % own] * scale

    def drain(g, _):
        couple(g).wait_send()
        pool(g).wait_send()
        hand(g).wait_send()
        for k in range(1, pairs):
            exchange(g, k).wait_send()
        return 0

    lax.fori_loop(0, groups, drain, 0)
    for k in range(1, pairs):
        scatter(k).wait_send()
        gather(k).wait_send()
    for k in range(pairs):
        forward(k).wait_send()


def per_device(n, ntp, grad_out, query_in, key_in, value_in, residue, log_rate):
    rows, chans = grad_out.shape
    modes = residue.shape[1]
    span = rows // SUB
    chunks = chans // LANES
    pairs = n // 2
    groups = GROUPS if chunks % (2 * GROUPS) == 0 and n <= 32 else 1
    width = chans // groups
    half = width // 2
    own = -(-(chunks // 2 * 2 * modes // SUB) // pairs)
    f32 = jnp.float32
    shape = jax.ShapeDtypeStruct
    hbm = pl.BlockSpec(memory_space=pltpu.HBM)
    vmem = pl.BlockSpec(memory_space=pltpu.VMEM)
    buffer = lambda *dims: pltpu.VMEM(dims, f32)
    tile = lambda *lead: pltpu.VMEM((*lead, SUB, LANES), f32)
    flags = lambda *dims: pltpu.SemaphoreType.DMA(dims)
    wide_out = pltpu.VMEM((rows, chans), f32)
    filtered, back_filtered, d_res, d_rate = pl.pallas_call(
        functools.partial(fused_kernel, n, ntp, modes, groups),
        out_shape=(wide_out,) * 2 + (pltpu.VMEM((modes, chans), f32),) * 2,
        in_specs=[hbm] * 6,
        out_specs=(vmem,) * 4,
        scratch_shapes=[
            *[pltpu.VMEM((rows, chans), grad_out.dtype)] * 4,
            buffer(modes, chans),
            buffer(modes, chans),
            buffer(chunks, rows, LANES),
            buffer(chunks, rows, LANES),
            buffer(chunks, 2, modes * SUB, LANES),
            buffer(chunks, 2, SUB, modes, LANES),
            buffer(groups, 2, 4, modes, half),
            buffer(2, modes * SUB, LANES),
            buffer(2 * span * SUB, LANES),
            buffer(span, LANES),
            buffer((span + 1) * modes, LANES),
            buffer(rows, LANES),
            buffer(rows, LANES),
            buffer(groups, 2, 2, modes, half),
            buffer(groups, 2, modes, half),
            buffer(groups, 4, modes, half),
            buffer(groups, 2, modes, half),
            buffer(groups, pairs - 1, modes, half),
            buffer(groups, 2, 2, modes, half),
            buffer(groups, 2, modes, half),
            tile(own * pairs),
            tile(pairs - 1, own),
            tile(own),
            tile(2, pairs, own),
            tile(2 * ntp),
            flags(4, groups), flags(2),
            flags(groups), flags(groups),
            flags(groups), flags(groups),
            flags(groups, pairs - 1), flags(groups, pairs - 1),
            flags(groups), flags(groups),
            flags(pairs - 1), flags(pairs - 1),
            flags(pairs - 1), flags(pairs - 1),
            flags(pairs), flags(pairs),
            flags(2 * ntp - 1), flags(2 * ntp - 1),
        ],
        compiler_params=pltpu.CompilerParams(
            collective_id=0, has_side_effects=True, vmem_limit_bytes=VMEM_BYTES
        ),
        name="fused",
    )(grad_out, query_in, key_in, value_in, log_rate.T, residue.T)
    grad_query = (grad_out.astype(f32) * filtered).astype(jnp.bfloat16)
    grad_key = (back_filtered * value_in.astype(f32)).astype(jnp.bfloat16)
    grad_value = (back_filtered * key_in.astype(f32)).astype(jnp.bfloat16)
    return grad_query, grad_key, grad_value, d_res.T, d_rate.T


def solution(mesh):
    wide = P("ctx", "tp")
    tall = P("tp", None)
    body = functools.partial(per_device, mesh.shape["ctx"], mesh.shape["tp"])
    return jax.shard_map(
        body,
        mesh=mesh,
        in_specs=(wide,) * 4 + (tall,) * 2,
        out_specs=(wide,) * 3 + (tall,) * 2,
        check_vma=False,
    )
```

```python
import functools

import jax
import jax.numpy as jnp
from jax import lax
from jax.experimental import pallas as pl
from jax.experimental.pallas import tpu as pltpu
from jax.sharding import PartitionSpec as P

CLIP_NORM = 512
SUB = 8
LANES = 128
MESH = pl.DeviceIdType.MESH
VMEM_BYTES = 56 * 1024 * 1024
GROUPS = 4
JOIN_STEP = 2
JOIN_AT = -1
AHEAD = 2
FINISH_AT = 2
PASS_AT = 6


def total_of(terms):
    while len(terms) > 1:
        paired = [x + y for x, y in zip(terms[::2], terms[1::2])]
        terms = paired + ([terms[-1]] if len(terms) % 2 else [])
    return terms[0]


def fused_kernel(
    n, ntp, modes, groups,
    go_in, q_in, k_in, v_in, lr_in, res_in,
    for_ref, back_ref, dres_ref, drate_ref, scale_ref,
    go_ref, q_ref, k_ref, v_ref, lr_ref, res_ref,
    p_s, g_s, ends_s, pre_s, loc_s, turn_s, lag_s, hold_s, table, fr_s, br_s,
    ea_s, mate, mate_loc, pt_s, held, ca_s, back_s, raw_s, parts, red, gath, sums, squares,
    in_sem, small_sem, pa_send, pa_recv, pl_send, pl_recv, ex_send, ex_recv, bk_send, bk_recv,
    rs_send, rs_recv, ag_send, ag_recv, fw_send, fw_recv, sq_send, sq_recv,
):
    me = lax.axis_index("ctx")
    col = lax.axis_index("tp")
    pair = me // 2
    odd = lax.rem(me, 2)
    pairs = n // 2
    plane = 2 * ntp
    here = odd * ntp + col
    rows, chans = go_ref.shape
    span = rows // SUB
    width = chans // groups
    half = width // 2
    chunks = chans // LANES
    per_group = width // LANES
    per_half = half // LANES
    pieces = 2 * modes // SUB
    own = red.shape[1]
    zero = jnp.zeros((SUB, LANES), jnp.float32)
    folds = modes // SUB

    def fetch(which, g):
        at = pl.ds(pl.multiple_of(g * width, LANES), width)
        source = (go_in, q_in, k_in, v_in)[which]
        target = (go_ref, q_ref, k_ref, v_ref)[which]
        return pltpu.make_async_copy(source.at[:, at], target.at[:, at], in_sem.at[which, g])

    rate_copy = pltpu.make_async_copy(lr_in, lr_ref, small_sem.at[0])
    residue_copy = pltpu.make_async_copy(res_in, res_ref, small_sem.at[1])
    rate_copy.start()
    for g in range(groups):
        for which in (2, 3, 0, 1):
            fetch(which, g).start()
    residue_copy.start()

    def beside(q):
        other = lax.rem(here + q, plane)
        return {"ctx": pair * 2 + other // ntp, "tp": lax.rem(other, ntp)}

    def along(k):
        return {"ctx": lax.rem(pair + k, pairs) * 2 + odd}

    across_pair = {"ctx": pair * 2 + 1 - odd}
    barrier = pltpu.get_barrier_semaphore()
    for q in range(1, plane):
        pl.semaphore_signal(barrier, inc=1, device_id=beside(q), device_id_type=MESH)
    for k in range(1, pairs):
        pl.semaphore_signal(barrier, inc=1, device_id=along(k), device_id_type=MESH)

    def wide(x, m):
        return jnp.broadcast_to(x[m : m + 1], (SUB, LANES))

    def lanes(ch):
        return pl.ds(pl.multiple_of(ch * LANES, LANES), LANES)

    def fold(f):
        return pl.ds(f * SUB, SUB)

    def turned(q, f):
        return pl.ds(f * SUB * SUB + q, SUB, stride=SUB)

    def copy_to(source, target, send, recv, place):
        return pltpu.make_async_remote_copy(
            src_ref=source, dst_ref=target, send_sem=send, recv_sem=recv, device_id=place, device_id_type=MESH
        )

    def ends(ch):
        g, c = ch // per_group, lax.rem(ch, per_group)
        at = lanes(ch)
        p_s[ch] = k_ref[:, at].astype(jnp.float32) * v_ref[:, at].astype(jnp.float32)
        g_s[ch] = go_ref[:, at].astype(jnp.float32) * q_ref[:, at].astype(jnp.float32)
        rate = jnp.exp(lr_ref[:, at])
        decay = jnp.exp(-rate)
        for first in range(0, modes, 8):
            group = range(first, min(modes, first + 8))
            a = [wide(decay, m) for m in group]
            s = [zero] * len(a)
            t = [zero] * len(a)
            for i in range(span):
                x = p_s[ch, pl.ds(i, SUB, stride=span), :]
                y = g_s[ch, pl.ds(span - 1 - i, SUB, stride=span), :]
                s = [aa * ss + x for aa, ss in zip(a, s)]
                t = [aa * tt + y for aa, tt in zip(a, t)]
            for slot, m in enumerate(group):
                ends_s[ch, 0, m * SUB : (m + 1) * SUB] = s[slot]
                ends_s[ch, 1, m * SUB : (m + 1) * SUB] = t[slot]
        far = jnp.exp(-rate * span)
        side, inner = c // per_half, lanes(lax.rem(c, per_half))
        for f in range(folds):
            step = far[f * SUB : (f + 1) * SUB]
            s = zero
            t = zero
            for q in range(SUB):
                pre_s[ch, 0, q, fold(f)] = s
                s = step * s + ends_s[ch, 0, turned(q, f)]
                pre_s[ch, 1, SUB - 1 - q, fold(f)] = t
                t = step * t + ends_s[ch, 1, turned(SUB - 1 - q, f)]
            ea_s[g, side, 0, fold(f), inner] = s
            ea_s[g, side, 1, fold(f), inner] = t

    def local(ch):
        g, c = ch // per_group, lax.rem(ch, per_group)
        side, inner = c // per_half, lanes(lax.rem(c, per_half))
        rate = jnp.exp(lr_ref[:, lanes(ch)])
        decay = jnp.exp(-rate)
        power = decay
        for k in range(1, span + 1):
            table[k * modes : (k + 1) * modes] = power * float(k)
            power = power * decay
        x = [p_s[ch, pl.ds(b, SUB, stride=span), :] for b in range(span)]
        y = [g_s[ch, pl.ds(b, SUB, stride=span), :] for b in range(span)]
        for m in range(modes):
            da, de = [], []
            for k in range(1, span + 1):
                coeff = jnp.broadcast_to(table[k * modes + m : k * modes + m + 1], (SUB, LANES))
                da.append(coeff * y[k - 1])
                if k < span:
                    de.append(coeff * x[span - 1 - k])
                if len(da) == 4:
                    da = [total_of(da)]
                if len(de) == 4:
                    de = [total_of(de)]
            turn_s[0, m * SUB : (m + 1) * SUB] = total_of(da)
            turn_s[1, m * SUB : (m + 1) * SUB] = total_of(de)
        for j in range(span):
            terms = []
            for b in range(span - j):
                terms.append(y[b + j] * x[b])
                if len(terms) == 4:
                    terms = [total_of(terms)]
            lag_s[j * SUB : (j + 1) * SUB] = total_of(terms)
        for f in range(span // SUB):
            hold_s[f * SUB : (f + 1) * SUB] = total_of([lag_s[turned(q, f)] for q in range(SUB)])
        far = jnp.exp(-rate * span)
        for f in range(folds):
            a = decay[f * SUB : (f + 1) * SUB]
            step = far[f * SUB : (f + 1) * SUB]
            v = zero
            d = zero
            for j in reversed(range(span)):
                d = a * d + v
                v = a * v + jnp.broadcast_to(hold_s[j : j + 1], (SUB, LANES))
            z = a * step * float(span)
            raw = zero
            lag = zero
            ahead = zero
            behind = zero
            for q in range(SUB):
                before = pre_s[ch, 0, q, fold(f)]
                after = pre_s[ch, 1, q, fold(f)]
                u = turn_s[0, turned(q, f)] + z * after
                w = a * turn_s[1, turned(q, f)]
                raw = raw + before * ends_s[ch, 1, turned(q, f)]
                lag = lag + before * u + after * w
                behind = step * behind + w + z * before
            for q in reversed(range(SUB)):
                u = turn_s[0, turned(q, f)] + z * pre_s[ch, 1, q, fold(f)]
                ahead = step * ahead + u
            loc_s[g, side, 0, fold(f), inner] = v + a * raw
            loc_s[g, side, 1, fold(f), inner] = a * d + lag
            loc_s[g, side, 2, fold(f), inner] = ahead
            loc_s[g, side, 3, fold(f), inner] = behind

    def couple(g):
        return copy_to(ea_s.at[g, 1 - odd], mate.at[g], pa_send.at[g], pa_recv.at[g], across_pair)

    def pool(g):
        return copy_to(loc_s.at[g, 1 - odd], mate_loc.at[g], pl_send.at[g], pl_recv.at[g], across_pair)

    def exchange(g, k):
        there = lax.rem(pair + k, pairs)
        which = jnp.where(there < pair, 1, 0)
        return copy_to(
            pt_s.at[g, which], held.at[g, k - 1], ex_send.at[g, k - 1], ex_recv.at[g, k - 1], along(k)
        )

    def hand(g):
        return copy_to(back_s.at[g], ca_s.at[g, odd], bk_send.at[g], bk_recv.at[g], across_pair)

    def scatter(g, k):
        there = lax.rem(pair + k, pairs)
        return copy_to(
            raw_s.at[g, pl.ds(there * own, own)],
            parts.at[g, k - 1], rs_send.at[g, k - 1], rs_recv.at[g, k - 1], along(k),
        )

    def gather(g, k):
        return copy_to(red.at[g], gath.at[g, odd, pair], ag_send.at[g, k - 1], ag_recv.at[g, k - 1], along(k))

    def forward(g):
        return copy_to(gath.at[g, odd], gath.at[g, odd], fw_send.at[g], fw_recv.at[g], across_pair)

    def norm(q):
        return copy_to(squares.at[here], squares.at[here], sq_send.at[q - 1], sq_recv.at[q - 1], beside(q))

    def rates(g):
        at = pl.ds(pl.multiple_of(g * width + odd * half, LANES), half)
        return jnp.exp(lr_ref[:, at])

    def ordered(g):
        mine, other = ea_s[g, odd], mate[g]
        return jnp.where(odd == 1, other, mine), jnp.where(odd == 1, mine, other)

    def join(g):
        couple(g).wait_recv()
        across = jnp.exp(-rates(g) * rows)
        early, late = ordered(g)
        pt_s[g, 0] = across * early[0] + late[0]
        pt_s[g, 1] = early[1] + across * late[1]
        for k in range(1, pairs):
            exchange(g, k).start()

    def carry(g):
        rate = rates(g)
        back_s[g] = jnp.zeros_like(back_s[g])
        for k in range(1, pairs):
            exchange(g, k).wait_recv()
            origin = lax.rem(pair - k + pairs, pairs)
            which = jnp.where(origin < pair, 0, 1)
            gap = jnp.where(origin < pair, pair - origin, origin - pair) - 1
            power = jnp.exp(-rate * (gap * (2 * rows)).astype(jnp.float32))
            back_s[g, which] += power * held[g, k - 1]
        across = jnp.exp(-rate * rows)
        early, late = ordered(g)
        from_past = back_s[g, 0]
        from_next = back_s[g, 1]
        past = from_past, early[0] + across * from_past
        ahead = late[1] + across * from_next, from_next
        ca_s[g, odd, 0] = jnp.where(odd == 1, past[1], past[0])
        ca_s[g, odd, 1] = jnp.where(odd == 1, ahead[1], ahead[0])
        back_s[g, 0] = jnp.where(odd == 1, past[0], past[1])
        back_s[g, 1] = jnp.where(odd == 1, ahead[0], ahead[1])
        hand(g).start()

    def grads(g, c):
        inner = lanes(c)
        at = pl.ds(pl.multiple_of(g * width + odd * half + c * LANES, LANES), LANES)
        rate = jnp.exp(lr_ref[:, at])
        decay = jnp.exp(-rate)
        root = jnp.sqrt(2.0 * rate)
        weight = res_ref[:, at] * root
        through = jnp.exp(-rate * (rows + 1)) * float(rows)
        raw, lag = [], []
        for loc, past, ahead, first in (
            (loc_s.at[g, odd], ca_s[g, odd, 0, :, inner], ca_s[g, odd, 1, :, inner], ea_s[g, odd, 1, :, inner]),
            (mate_loc.at[g], back_s[g, 0, :, inner], back_s[g, 1, :, inner], mate[g, 1, :, inner]),
        ):
            raw.append(loc[0, :, inner] + decay * (past * first))
            lag.append(
                loc[1, :, inner] + past * loc[2, :, inner] + ahead * (loc[3, :, inner] + through * past)
            )
        raw_weight = raw[0] + raw[1]
        both = (root * raw_weight, weight * (0.5 * raw_weight - rate * (lag[0] + lag[1])))
        for piece in range(pieces):
            low = piece % (pieces // 2) * SUB
            raw_s[g, c * pieces + piece] = both[piece // (pieces // 2)][low : low + SUB]

    def reduce_start(g):
        carry(g)
        pool(g).wait_recv()
        for c in range(per_half):
            grads(g, c)
        for k in range(1, pairs):
            scatter(g, k).start()

    def reduce_finish(g):
        mine = raw_s[g, pl.ds(pair * own, own)]
        for k in range(1, pairs):
            scatter(g, k).wait_recv()
            mine = mine + parts[g, k - 1]
        red[g] = mine
        for k in range(1, pairs):
            gather(g, k).start()
        gath[g, odd, pair] = mine

    def unpack(g, side):
        for c in range(per_half):
            at = pl.ds(pl.multiple_of(g * width + side * half + c * LANES, LANES), LANES)
            for piece in range(pieces):
                tile = c * pieces + piece
                low = piece % (pieces // 2) * SUB
                ref = dres_ref if piece < pieces // 2 else drate_ref
                ref[low : low + SUB, at] = gath[g, side, tile // own, tile % own]

    def pass_on(g):
        for k in range(1, pairs):
            gather(g, k).wait_recv()
        forward(g).start()
        whole = gath[g, odd]
        sums[...] += jnp.sum(jnp.sum(whole * whole, axis=0), axis=0)
        unpack(g, odd)

    def filters(ch):
        g, c = ch // per_group, lax.rem(ch, per_group)
        side, inner = c // per_half, lanes(lax.rem(c, per_half))
        at = lanes(ch)
        rate = jnp.exp(lr_ref[:, at])
        decay = jnp.exp(-rate)
        far = jnp.exp(-rate * span)
        for f in range(folds):
            step = far[f * SUB : (f + 1) * SUB]
            past = ca_s[g, side, 0, fold(f), inner]
            ahead = ca_s[g, side, 1, fold(f), inner]
            for q in range(SUB):
                turn_s[0, turned(q, f)] = pre_s[ch, 0, q, fold(f)] + past
                turn_s[1, turned(SUB - 1 - q, f)] = pre_s[ch, 1, SUB - 1 - q, fold(f)] + ahead
                past = step * past
                ahead = step * ahead
        power = res_ref[:, at] * jnp.sqrt(2.0 * rate)
        for k in range(span + 1):
            table[k * modes : (k + 1) * modes] = power
            power = power * decay
        for f in range(span // SUB):
            hold_s[f * SUB : (f + 1) * SUB] = total_of(
                [table[pl.ds(f * SUB * modes + m, SUB, stride=modes)] for m in range(modes)]
            )
        h = [jnp.broadcast_to(hold_s[j : j + 1], (SUB, LANES)) for j in range(span)]
        x = [p_s[ch, pl.ds(b, SUB, stride=span), :] for b in range(span)]
        for b in range(span):
            terms = []
            for j in range(b + 1):
                terms.append(h[j] * x[b - j])
                if len(terms) == 4:
                    terms = [total_of(terms)]
            lag_s[b * SUB : (b + 1) * SUB] = total_of(terms)
        y = [g_s[ch, pl.ds(b, SUB, stride=span), :] for b in range(span)]
        for b in range(span):
            terms = []
            for j in range(span - b):
                terms.append(h[j] * y[b + j])
                if len(terms) == 4:
                    terms = [total_of(terms)]
            lag_s[(span + b) * SUB : (span + b + 1) * SUB] = total_of(terms)
        s = [turn_s[0, m * SUB : (m + 1) * SUB] for m in range(modes)]
        t = [turn_s[1, m * SUB : (m + 1) * SUB] for m in range(modes)]
        for k in range(1, span + 1):
            b = k - 1
            r = span - k
            fore = [lag_s[b * SUB : (b + 1) * SUB]]
            back = [lag_s[(span + r) * SUB : (span + r + 1) * SUB]]
            for m in range(modes):
                coeff = jnp.broadcast_to(table[k * modes + m : k * modes + m + 1], (SUB, LANES))
                fore.append(coeff * s[m])
                back.append(coeff * t[m])
                if len(fore) == 4:
                    fore = [total_of(fore)]
                    back = [total_of(back)]
            fr_s[pl.ds(b, SUB, stride=span), :] = total_of(fore)
            br_s[pl.ds(r, SUB, stride=span), :] = total_of(back)
        for_ref[:, at] = fr_s[...]
        back_ref[:, at] = br_s[...]

    if raw_s.shape[1] > per_half * pieces:
        raw_s[...] = jnp.zeros_like(raw_s)

    def order(i):
        later = i // (chunks // 2)
        j = lax.rem(i, chunks // 2)
        g, c = j // per_half, lax.rem(j, per_half)
        side = jnp.where(later == 1, odd, 1 - odd)
        return later, g, c, g * per_group + side * per_half + c

    def first_stage(i, _):
        later, g, c, ch = order(i)

        @pl.when((later == 0) & (c == 0))
        def _():
            for which in range(4):
                fetch(which, g).wait()

        ends(ch)

        @pl.when(i == per_half - 1)
        def _():
            pl.semaphore_wait(barrier, plane + pairs - 2)

        @pl.when((later == 0) & (c == per_half - 1))
        def _():
            couple(g).start()

        return 0

    def second_stage(i, _):
        later, g, c, ch = order(i)
        for h in range(groups):
            pl.when(i == max(JOIN_STEP * h + JOIN_AT, 0))(functools.partial(join, h))
        local(ch)

        @pl.when((later == 0) & (c == per_half - 1))
        def _():
            pool(g).start()

        return 0

    def third_stage(i, _):
        theirs = i // groups
        g = lax.rem(i, groups)

        @pl.when(theirs == 1)
        def _():
            hand(g).wait_recv()

        def one(c, _):
            side = jnp.where(theirs == 1, 1 - odd, odd)
            filters(g * per_group + side * per_half + c)
            return 0

        lax.fori_loop(0, per_half, one, 0)
        for h in range(groups):
            if h >= AHEAD:
                pl.when(i == h - AHEAD)(functools.partial(reduce_start, h))
        for h in range(groups):
            pl.when(i == min(h + FINISH_AT, last))(functools.partial(reduce_finish, h))
        for h in range(groups):
            pl.when(i == min(h + PASS_AT, last))(functools.partial(pass_on, h))
        return 0

    last = 2 * groups - 1
    sums[...] = zero
    rate_copy.wait()
    lax.fori_loop(0, chunks, first_stage, 0)
    residue_copy.wait()
    lax.fori_loop(0, chunks, second_stage, 0)
    for g in range(min(AHEAD, groups)):
        reduce_start(g)
    lax.fori_loop(0, 2 * groups, third_stage, 0)
    squares[here] = sums[...]
    for q in range(1, plane):
        norm(q).start()
    for g in range(groups):
        forward(g).wait_recv()
        unpack(g, 1 - odd)
    for q in range(1, plane):
        norm(q).wait()
    square = jnp.sum(jnp.sum(squares[...], axis=0), keepdims=True)
    scale = jnp.minimum(1.0, CLIP_NORM / jnp.sqrt(square + 1e-06))
    scale_ref[...] = jnp.broadcast_to(scale, scale_ref.shape)

    def drain(g, _):
        couple(g).wait_send()
        pool(g).wait_send()
        hand(g).wait_send()
        forward(g).wait_send()
        for k in range(1, pairs):
            exchange(g, k).wait_send()
            scatter(g, k).wait_send()
            gather(g, k).wait_send()
        return 0

    lax.fori_loop(0, groups, drain, 0)


def per_device(n, ntp, grad_out, query_in, key_in, value_in, residue, log_rate):
    rows, chans = grad_out.shape
    modes = residue.shape[1]
    span = rows // SUB
    chunks = chans // LANES
    pairs = n // 2
    groups = GROUPS if chunks % (2 * GROUPS) == 0 and n <= 32 else 1
    width = chans // groups
    half = width // 2
    own = -(-(half // LANES * 2 * modes // SUB) // pairs)
    f32 = jnp.float32
    shape = jax.ShapeDtypeStruct
    hbm = pl.BlockSpec(memory_space=pltpu.HBM)
    vmem = pl.BlockSpec(memory_space=pltpu.VMEM)
    buffer = lambda *dims: pltpu.VMEM(dims, f32)
    tile = lambda *lead: pltpu.VMEM((*lead, SUB, LANES), f32)
    flags = lambda *dims: pltpu.SemaphoreType.DMA(dims)
    wide_out = pltpu.VMEM((rows, chans), f32)
    filtered, back_filtered, d_res, d_rate, scale = pl.pallas_call(
        functools.partial(fused_kernel, n, ntp, modes, groups),
        out_shape=(wide_out,) * 2 + (pltpu.VMEM((modes, chans), f32),) * 3,
        in_specs=[hbm] * 6,
        out_specs=(vmem,) * 5,
        scratch_shapes=[
            *[pltpu.VMEM((rows, chans), grad_out.dtype)] * 4,
            buffer(modes, chans),
            buffer(modes, chans),
            buffer(chunks, rows, LANES),
            buffer(chunks, rows, LANES),
            buffer(chunks, 2, modes * SUB, LANES),
            buffer(chunks, 2, SUB, modes, LANES),
            buffer(groups, 2, 4, modes, half),
            buffer(2, modes * SUB, LANES),
            buffer(2 * span * SUB, LANES),
            buffer(span, LANES),
            buffer((span + 1) * modes, LANES),
            buffer(rows, LANES),
            buffer(rows, LANES),
            buffer(groups, 2, 2, modes, half),
            buffer(groups, 2, modes, half),
            buffer(groups, 4, modes, half),
            buffer(groups, 2, modes, half),
            buffer(groups, pairs - 1, modes, half),
            buffer(groups, 2, 2, modes, half),
            buffer(groups, 2, modes, half),
            tile(groups, own * pairs),
            tile(groups, pairs - 1, own),
            tile(groups, own),
            tile(groups, 2, pairs, own),
            tile(),
            tile(2 * ntp),
            flags(4, groups), flags(2),
            flags(groups), flags(groups),
            flags(groups), flags(groups),
            flags(groups, pairs - 1), flags(groups, pairs - 1),
            flags(groups), flags(groups),
            flags(groups, pairs - 1), flags(groups, pairs - 1),
            flags(groups, pairs - 1), flags(groups, pairs - 1),
            flags(groups), flags(groups),
            flags(2 * ntp - 1), flags(2 * ntp - 1),
        ],
        compiler_params=pltpu.CompilerParams(
            collective_id=0, has_side_effects=True, vmem_limit_bytes=VMEM_BYTES
        ),
        name="fused",
    )(grad_out, query_in, key_in, value_in, log_rate.T, residue.T)
    grad_query = (grad_out.astype(f32) * filtered).astype(jnp.bfloat16)
    grad_key = (back_filtered * value_in.astype(f32)).astype(jnp.bfloat16)
    grad_value = (back_filtered * key_in.astype(f32)).astype(jnp.bfloat16)
    return grad_query, grad_key, grad_value, (d_res * scale).T, (d_rate * scale).T


def solution(mesh):
    wide = P("ctx", "tp")
    tall = P("tp", None)
    body = functools.partial(per_device, mesh.shape["ctx"], mesh.shape["tp"])
    return jax.shard_map(
        body,
        mesh=mesh,
        in_specs=(wide,) * 4 + (tall,) * 2,
        out_specs=(wide,) * 3 + (tall,) * 2,
        check_vma=False,
    )
```

```python
import functools

import jax
import jax.numpy as jnp
from jax import lax
from jax.experimental import pallas as pl
from jax.experimental.pallas import tpu as pltpu
from jax.sharding import PartitionSpec as P

CLIP_NORM = 512
SUB = 8
LANES = 128
MESH = pl.DeviceIdType.MESH
VMEM_BYTES = 56 * 1024 * 1024
GROUPS = 4
LAG = 2
REST = 4


def total_of(terms):
    while len(terms) > 1:
        paired = [x + y for x, y in zip(terms[::2], terms[1::2])]
        terms = paired + ([terms[-1]] if len(terms) % 2 else [])
    return terms[0]


def fused_kernel(
    n, ntp, modes, groups,
    go_in, q_in, k_in, v_in, lr_in, res_in,
    for_ref, back_ref, dres_ref, drate_ref, scale_ref,
    go_ref, q_ref, k_ref, v_ref, lr_ref, res_ref,
    p_s, g_s, ends_s, pre_s, loc_s, turn_s, lag_s, hold_s, table, fr_s, br_s,
    ea_s, mate, mate_loc, pt_s, held, ca_s, back_s, raw_s, parts, red, gath, sums, squares,
    in_sem, small_sem, pa_send, pa_recv, pl_send, pl_recv, ex_send, ex_recv, bk_send, bk_recv,
    rs_send, rs_recv, ag_send, ag_recv, fw_send, fw_recv, sq_send, sq_recv,
):
    me = lax.axis_index("ctx")
    col = lax.axis_index("tp")
    pair = me // 2
    odd = lax.rem(me, 2)
    pairs = n // 2
    plane = 2 * ntp
    here = odd * ntp + col
    rows, chans = go_ref.shape
    span = rows // SUB
    width = chans // groups
    half = width // 2
    chunks = chans // LANES
    per_group = width // LANES
    per_half = half // LANES
    pieces = 2 * modes // SUB
    own = red.shape[1]
    zero = jnp.zeros((SUB, LANES), jnp.float32)
    folds = modes // SUB

    def fetch(which, g):
        at = pl.ds(pl.multiple_of(g * width, LANES), width)
        source = (go_in, q_in, k_in, v_in)[which]
        target = (go_ref, q_ref, k_ref, v_ref)[which]
        return pltpu.make_async_copy(source.at[:, at], target.at[:, at], in_sem.at[which, g])

    rate_copy = pltpu.make_async_copy(lr_in, lr_ref, small_sem.at[0])
    residue_copy = pltpu.make_async_copy(res_in, res_ref, small_sem.at[1])
    rate_copy.start()
    for g in range(groups):
        for which in (2, 3, 0, 1):
            fetch(which, g).start()
    residue_copy.start()

    def beside(q):
        other = lax.rem(here + q, plane)
        return {"ctx": pair * 2 + other // ntp, "tp": lax.rem(other, ntp)}

    def along(k):
        return {"ctx": lax.rem(pair + k, pairs) * 2 + odd}

    across_pair = {"ctx": pair * 2 + 1 - odd}
    barrier = pltpu.get_barrier_semaphore()
    for q in range(1, plane):
        pl.semaphore_signal(barrier, inc=1, device_id=beside(q), device_id_type=MESH)
    for k in range(1, pairs):
        pl.semaphore_signal(barrier, inc=1, device_id=along(k), device_id_type=MESH)

    def wide(x, m):
        return jnp.broadcast_to(x[m : m + 1], (SUB, LANES))

    def lanes(ch):
        return pl.ds(pl.multiple_of(ch * LANES, LANES), LANES)

    def fold(f):
        return pl.ds(f * SUB, SUB)

    def turned(q, f):
        return pl.ds(f * SUB * SUB + q, SUB, stride=SUB)

    def copy_to(source, target, send, recv, place):
        return pltpu.make_async_remote_copy(
            src_ref=source, dst_ref=target, send_sem=send, recv_sem=recv, device_id=place, device_id_type=MESH
        )

    def ends(ch):
        g, c = ch // per_group, lax.rem(ch, per_group)
        at = lanes(ch)
        p_s[ch] = k_ref[:, at].astype(jnp.float32) * v_ref[:, at].astype(jnp.float32)
        g_s[ch] = go_ref[:, at].astype(jnp.float32) * q_ref[:, at].astype(jnp.float32)
        rate = jnp.exp(lr_ref[:, at])
        decay = jnp.exp(-rate)
        for first in range(0, modes, 8):
            group = range(first, min(modes, first + 8))
            a = [wide(decay, m) for m in group]
            s = [zero] * len(a)
            t = [zero] * len(a)
            for i in range(span):
                x = p_s[ch, pl.ds(i, SUB, stride=span), :]
                y = g_s[ch, pl.ds(span - 1 - i, SUB, stride=span), :]
                s = [aa * ss + x for aa, ss in zip(a, s)]
                t = [aa * tt + y for aa, tt in zip(a, t)]
            for slot, m in enumerate(group):
                ends_s[ch, 0, m * SUB : (m + 1) * SUB] = s[slot]
                ends_s[ch, 1, m * SUB : (m + 1) * SUB] = t[slot]
        far = jnp.exp(-rate * span)
        side, inner = c // per_half, lanes(lax.rem(c, per_half))
        for f in range(folds):
            step = far[f * SUB : (f + 1) * SUB]
            s = zero
            t = zero
            for q in range(SUB):
                pre_s[ch, 0, q, fold(f)] = s
                s = step * s + ends_s[ch, 0, turned(q, f)]
                pre_s[ch, 1, SUB - 1 - q, fold(f)] = t
                t = step * t + ends_s[ch, 1, turned(SUB - 1 - q, f)]
            ea_s[g, side, 0, fold(f), inner] = s
            ea_s[g, side, 1, fold(f), inner] = t

    def local(ch):
        g, c = ch // per_group, lax.rem(ch, per_group)
        side, inner = c // per_half, lanes(lax.rem(c, per_half))
        rate = jnp.exp(lr_ref[:, lanes(ch)])
        decay = jnp.exp(-rate)
        power = decay
        for k in range(1, span + 1):
            table[k * modes : (k + 1) * modes] = power * float(k)
            power = power * decay
        x = [p_s[ch, pl.ds(b, SUB, stride=span), :] for b in range(span)]
        y = [g_s[ch, pl.ds(b, SUB, stride=span), :] for b in range(span)]
        for m in range(modes):
            da, de = [], []
            for k in range(1, span + 1):
                coeff = jnp.broadcast_to(table[k * modes + m : k * modes + m + 1], (SUB, LANES))
                da.append(coeff * y[k - 1])
                if k < span:
                    de.append(coeff * x[span - 1 - k])
                if len(da) == 4:
                    da = [total_of(da)]
                if len(de) == 4:
                    de = [total_of(de)]
            turn_s[0, m * SUB : (m + 1) * SUB] = total_of(da)
            turn_s[1, m * SUB : (m + 1) * SUB] = total_of(de)
        for j in range(span):
            terms = []
            for b in range(span - j):
                terms.append(y[b + j] * x[b])
                if len(terms) == 4:
                    terms = [total_of(terms)]
            lag_s[j * SUB : (j + 1) * SUB] = total_of(terms)
        for f in range(span // SUB):
            hold_s[f * SUB : (f + 1) * SUB] = total_of([lag_s[turned(q, f)] for q in range(SUB)])
        far = jnp.exp(-rate * span)
        for f in range(folds):
            a = decay[f * SUB : (f + 1) * SUB]
            step = far[f * SUB : (f + 1) * SUB]
            v = zero
            d = zero
            for j in reversed(range(span)):
                d = a * d + v
                v = a * v + jnp.broadcast_to(hold_s[j : j + 1], (SUB, LANES))
            z = a * step * float(span)
            raw = zero
            lag = zero
            ahead = zero
            behind = zero
            for q in range(SUB):
                before = pre_s[ch, 0, q, fold(f)]
                after = pre_s[ch, 1, q, fold(f)]
                u = turn_s[0, turned(q, f)] + z * after
                w = a * turn_s[1, turned(q, f)]
                raw = raw + before * ends_s[ch, 1, turned(q, f)]
                lag = lag + before * u + after * w
                behind = step * behind + w + z * before
            for q in reversed(range(SUB)):
                u = turn_s[0, turned(q, f)] + z * pre_s[ch, 1, q, fold(f)]
                ahead = step * ahead + u
            loc_s[g, side, 0, fold(f), inner] = v + a * raw
            loc_s[g, side, 1, fold(f), inner] = a * d + lag
            loc_s[g, side, 2, fold(f), inner] = ahead
            loc_s[g, side, 3, fold(f), inner] = behind

    def couple(g):
        return copy_to(ea_s.at[g, 1 - odd], mate.at[g], pa_send.at[g], pa_recv.at[g], across_pair)

    def pool(g):
        return copy_to(loc_s.at[g, 1 - odd], mate_loc.at[g], pl_send.at[g], pl_recv.at[g], across_pair)

    def exchange(g, k):
        there = lax.rem(pair + k, pairs)
        which = jnp.where(there < pair, 1, 0)
        return copy_to(
            pt_s.at[g, which], held.at[g, k - 1], ex_send.at[g, k - 1], ex_recv.at[g, k - 1], along(k)
        )

    def hand(g):
        return copy_to(back_s.at[g], ca_s.at[g, odd], bk_send.at[g], bk_recv.at[g], across_pair)

    def scatter(g, k):
        there = lax.rem(pair + k, pairs)
        return copy_to(
            raw_s.at[g, pl.ds(there * own, own)],
            parts.at[g, k - 1], rs_send.at[g, k - 1], rs_recv.at[g, k - 1], along(k),
        )

    def gather(g, k):
        return copy_to(red.at[g], gath.at[g, odd, pair], ag_send.at[g, k - 1], ag_recv.at[g, k - 1], along(k))

    def forward(g):
        return copy_to(gath.at[g, odd], gath.at[g, odd], fw_send.at[g], fw_recv.at[g], across_pair)

    def norm(q):
        return copy_to(squares.at[here], squares.at[here], sq_send.at[q - 1], sq_recv.at[q - 1], beside(q))

    def rates(g):
        at = pl.ds(pl.multiple_of(g * width + odd * half, LANES), half)
        return jnp.exp(lr_ref[:, at])

    def ordered(g):
        mine, other = ea_s[g, odd], mate[g]
        return jnp.where(odd == 1, other, mine), jnp.where(odd == 1, mine, other)

    def join(g):
        couple(g).wait_recv()
        across = jnp.exp(-rates(g) * rows)
        early, late = ordered(g)
        pt_s[g, 0] = across * early[0] + late[0]
        pt_s[g, 1] = early[1] + across * late[1]
        for k in range(1, pairs):
            exchange(g, k).start()

    def carry(g):
        rate = rates(g)
        back_s[g] = jnp.zeros_like(back_s[g])
        for k in range(1, pairs):
            exchange(g, k).wait_recv()
            origin = lax.rem(pair - k + pairs, pairs)
            which = jnp.where(origin < pair, 0, 1)
            gap = jnp.where(origin < pair, pair - origin, origin - pair) - 1
            power = jnp.exp(-rate * (gap * (2 * rows)).astype(jnp.float32))
            back_s[g, which] += power * held[g, k - 1]
        across = jnp.exp(-rate * rows)
        early, late = ordered(g)
        from_past = back_s[g, 0]
        from_next = back_s[g, 1]
        past = from_past, early[0] + across * from_past
        ahead = late[1] + across * from_next, from_next
        ca_s[g, odd, 0] = jnp.where(odd == 1, past[1], past[0])
        ca_s[g, odd, 1] = jnp.where(odd == 1, ahead[1], ahead[0])
        back_s[g, 0] = jnp.where(odd == 1, past[0], past[1])
        back_s[g, 1] = jnp.where(odd == 1, ahead[0], ahead[1])
        hand(g).start()

    def grads(g, c):
        inner = lanes(c)
        at = pl.ds(pl.multiple_of(g * width + odd * half + c * LANES, LANES), LANES)
        rate = jnp.exp(lr_ref[:, at])
        decay = jnp.exp(-rate)
        root = jnp.sqrt(2.0 * rate)
        weight = res_ref[:, at] * root
        through = jnp.exp(-rate * (rows + 1)) * float(rows)
        raw, lag = [], []
        for loc, past, ahead, first in (
            (loc_s.at[g, odd], ca_s[g, odd, 0, :, inner], ca_s[g, odd, 1, :, inner], ea_s[g, odd, 1, :, inner]),
            (mate_loc.at[g], back_s[g, 0, :, inner], back_s[g, 1, :, inner], mate[g, 1, :, inner]),
        ):
            raw.append(loc[0, :, inner] + decay * (past * first))
            lag.append(
                loc[1, :, inner] + past * loc[2, :, inner] + ahead * (loc[3, :, inner] + through * past)
            )
        raw_weight = raw[0] + raw[1]
        both = (root * raw_weight, weight * (0.5 * raw_weight - rate * (lag[0] + lag[1])))
        for piece in range(pieces):
            low = piece % (pieces // 2) * SUB
            raw_s[g, c * pieces + piece] = both[piece // (pieces // 2)][low : low + SUB]

    def reduce_start(g):
        carry(g)
        pool(g).wait_recv()
        for c in range(per_half):
            grads(g, c)
        for k in range(1, pairs):
            scatter(g, k).start()

    def reduce_finish(g):
        mine = raw_s[g, pl.ds(pair * own, own)]
        for k in range(1, pairs):
            scatter(g, k).wait_recv()
            mine = mine + parts[g, k - 1]
        red[g] = mine
        for k in range(1, pairs):
            gather(g, k).start()
        gath[g, odd, pair] = mine

    def unpack(g, side):
        for c in range(per_half):
            at = pl.ds(pl.multiple_of(g * width + side * half + c * LANES, LANES), LANES)
            for piece in range(pieces):
                tile = c * pieces + piece
                low = piece % (pieces // 2) * SUB
                ref = dres_ref if piece < pieces // 2 else drate_ref
                ref[low : low + SUB, at] = gath[g, side, tile // own, tile % own]

    def pass_on(g):
        for k in range(1, pairs):
            gather(g, k).wait_recv()
        forward(g).start()
        whole = gath[g, odd]
        sums[...] += jnp.sum(jnp.sum(whole * whole, axis=0), axis=0)
        unpack(g, odd)

    def filters(ch):
        g, c = ch // per_group, lax.rem(ch, per_group)
        side, inner = c // per_half, lanes(lax.rem(c, per_half))
        at = lanes(ch)
        rate = jnp.exp(lr_ref[:, at])
        decay = jnp.exp(-rate)
        far = jnp.exp(-rate * span)
        for f in range(folds):
            step = far[f * SUB : (f + 1) * SUB]
            past = ca_s[g, side, 0, fold(f), inner]
            ahead = ca_s[g, side, 1, fold(f), inner]
            for q in range(SUB):
                turn_s[0, turned(q, f)] = pre_s[ch, 0, q, fold(f)] + past
                turn_s[1, turned(SUB - 1 - q, f)] = pre_s[ch, 1, SUB - 1 - q, fold(f)] + ahead
                past = step * past
                ahead = step * ahead
        power = res_ref[:, at] * jnp.sqrt(2.0 * rate)
        for k in range(span + 1):
            table[k * modes : (k + 1) * modes] = power
            power = power * decay
        for f in range(span // SUB):
            hold_s[f * SUB : (f + 1) * SUB] = total_of(
                [table[pl.ds(f * SUB * modes + m, SUB, stride=modes)] for m in range(modes)]
            )
        h = [jnp.broadcast_to(hold_s[j : j + 1], (SUB, LANES)) for j in range(span)]
        x = [p_s[ch, pl.ds(b, SUB, stride=span), :] for b in range(span)]
        for b in range(span):
            terms = []
            for j in range(b + 1):
                terms.append(h[j] * x[b - j])
                if len(terms) == 4:
                    terms = [total_of(terms)]
            lag_s[b * SUB : (b + 1) * SUB] = total_of(terms)
        y = [g_s[ch, pl.ds(b, SUB, stride=span), :] for b in range(span)]
        for b in range(span):
            terms = []
            for j in range(span - b):
                terms.append(h[j] * y[b + j])
                if len(terms) == 4:
                    terms = [total_of(terms)]
            lag_s[(span + b) * SUB : (span + b + 1) * SUB] = total_of(terms)
        s = [turn_s[0, m * SUB : (m + 1) * SUB] for m in range(modes)]
        t = [turn_s[1, m * SUB : (m + 1) * SUB] for m in range(modes)]
        for k in range(1, span + 1):
            b = k - 1
            r = span - k
            fore = [lag_s[b * SUB : (b + 1) * SUB]]
            back = [lag_s[(span + r) * SUB : (span + r + 1) * SUB]]
            for m in range(modes):
                coeff = jnp.broadcast_to(table[k * modes + m : k * modes + m + 1], (SUB, LANES))
                fore.append(coeff * s[m])
                back.append(coeff * t[m])
                if len(fore) == 4:
                    fore = [total_of(fore)]
                    back = [total_of(back)]
            fr_s[pl.ds(b, SUB, stride=span), :] = total_of(fore)
            br_s[pl.ds(r, SUB, stride=span), :] = total_of(back)
        for_ref[:, at] = fr_s[...]
        back_ref[:, at] = br_s[...]

    if raw_s.shape[1] > per_half * pieces:
        raw_s[...] = jnp.zeros_like(raw_s)

    def part(g, theirs, c):
        return g * per_group + jnp.where(theirs, 1 - odd, odd) * per_half + c

    def each(act, g, theirs):
        def one(c, _):
            act(part(g, theirs, c))
            return 0

        lax.fori_loop(0, per_half, one, 0)

    def first_stage(g, _):
        for which in range(4):
            fetch(which, g).wait()
        each(ends, g, True)

        @pl.when(g == 0)
        def _():
            pl.semaphore_wait(barrier, plane + pairs - 2)

        couple(g).start()
        return 0

    def second_stage(g, _):
        each(local, g, True)
        pool(g).start()
        each(ends, g, False)
        join(g)
        return 0

    def start_at(h):
        return h + min(LAG, groups - 1)

    def finish_at(h):
        return min(start_at(h) + REST, 3 * groups - 1)

    def pass_at(h):
        return max(min(finish_at(h) + REST, 3 * groups - 1), groups)

    def third_stage(g, _):
        each(local, g, False)
        for h in range(groups):
            if start_at(h) < groups:
                pl.when(g == start_at(h))(functools.partial(reduce_start, h))
        return 0

    def fourth_stage(i, _):
        theirs = i // groups == 1
        g = lax.rem(i, groups)

        @pl.when(theirs)
        def _():
            hand(g).wait_recv()

        each(filters, g, theirs)
        for h in range(groups):
            if start_at(h) >= groups:
                pl.when(i == start_at(h) - groups)(functools.partial(reduce_start, h))
        for h in range(groups):
            pl.when(i == max(finish_at(h) - groups, 0))(functools.partial(reduce_finish, h))
        for h in range(groups):
            pl.when(i == pass_at(h) - groups)(functools.partial(pass_on, h))
        return 0

    sums[...] = zero
    rate_copy.wait()
    lax.fori_loop(0, groups, first_stage, 0)
    lax.fori_loop(0, groups, second_stage, 0)
    residue_copy.wait()
    lax.fori_loop(0, groups, third_stage, 0)
    lax.fori_loop(0, 2 * groups, fourth_stage, 0)
    squares[here] = sums[...]
    for q in range(1, plane):
        norm(q).start()
    for g in range(groups):
        forward(g).wait_recv()
        unpack(g, 1 - odd)
    for q in range(1, plane):
        norm(q).wait()
    square = jnp.sum(jnp.sum(squares[...], axis=0), keepdims=True)
    scale = jnp.minimum(1.0, CLIP_NORM / jnp.sqrt(square + 1e-06))
    scale_ref[...] = jnp.broadcast_to(scale, scale_ref.shape)

    def drain(g, _):
        couple(g).wait_send()
        pool(g).wait_send()
        hand(g).wait_send()
        forward(g).wait_send()
        for k in range(1, pairs):
            exchange(g, k).wait_send()
            scatter(g, k).wait_send()
            gather(g, k).wait_send()
        return 0

    lax.fori_loop(0, groups, drain, 0)


def per_device(n, ntp, grad_out, query_in, key_in, value_in, residue, log_rate):
    rows, chans = grad_out.shape
    modes = residue.shape[1]
    span = rows // SUB
    chunks = chans // LANES
    pairs = n // 2
    groups = GROUPS if chunks % (2 * GROUPS) == 0 and n <= 32 else 1
    width = chans // groups
    half = width // 2
    own = -(-(half // LANES * 2 * modes // SUB) // pairs)
    f32 = jnp.float32
    shape = jax.ShapeDtypeStruct
    hbm = pl.BlockSpec(memory_space=pltpu.HBM)
    vmem = pl.BlockSpec(memory_space=pltpu.VMEM)
    buffer = lambda *dims: pltpu.VMEM(dims, f32)
    tile = lambda *lead: pltpu.VMEM((*lead, SUB, LANES), f32)
    flags = lambda *dims: pltpu.SemaphoreType.DMA(dims)
    wide_out = pltpu.VMEM((rows, chans), f32)
    filtered, back_filtered, d_res, d_rate, scale = pl.pallas_call(
        functools.partial(fused_kernel, n, ntp, modes, groups),
        out_shape=(wide_out,) * 2 + (pltpu.VMEM((modes, chans), f32),) * 3,
        in_specs=[hbm] * 6,
        out_specs=(vmem,) * 5,
        scratch_shapes=[
            *[pltpu.VMEM((rows, chans), grad_out.dtype)] * 4,
            buffer(modes, chans),
            buffer(modes, chans),
            buffer(chunks, rows, LANES),
            buffer(chunks, rows, LANES),
            buffer(chunks, 2, modes * SUB, LANES),
            buffer(chunks, 2, SUB, modes, LANES),
            buffer(groups, 2, 4, modes, half),
            buffer(2, modes * SUB, LANES),
            buffer(2 * span * SUB, LANES),
            buffer(span, LANES),
            buffer((span + 1) * modes, LANES),
            buffer(rows, LANES),
            buffer(rows, LANES),
            buffer(groups, 2, 2, modes, half),
            buffer(groups, 2, modes, half),
            buffer(groups, 4, modes, half),
            buffer(groups, 2, modes, half),
            buffer(groups, pairs - 1, modes, half),
            buffer(groups, 2, 2, modes, half),
            buffer(groups, 2, modes, half),
            tile(groups, own * pairs),
            tile(groups, pairs - 1, own),
            tile(groups, own),
            tile(groups, 2, pairs, own),
            tile(),
            tile(2 * ntp),
            flags(4, groups), flags(2),
            flags(groups), flags(groups),
            flags(groups), flags(groups),
            flags(groups, pairs - 1), flags(groups, pairs - 1),
            flags(groups), flags(groups),
            flags(groups, pairs - 1), flags(groups, pairs - 1),
            flags(groups, pairs - 1), flags(groups, pairs - 1),
            flags(groups), flags(groups),
            flags(2 * ntp - 1), flags(2 * ntp - 1),
        ],
        compiler_params=pltpu.CompilerParams(
            collective_id=0, has_side_effects=True, vmem_limit_bytes=VMEM_BYTES
        ),
        name="fused",
    )(grad_out, query_in, key_in, value_in, log_rate.T, residue.T)
    grad_query = (grad_out.astype(f32) * filtered).astype(jnp.bfloat16)
    grad_key = (back_filtered * value_in.astype(f32)).astype(jnp.bfloat16)
    grad_value = (back_filtered * key_in.astype(f32)).astype(jnp.bfloat16)
    return grad_query, grad_key, grad_value, (d_res * scale).T, (d_rate * scale).T


def solution(mesh):
    wide = P("ctx", "tp")
    tall = P("tp", None)
    body = functools.partial(per_device, mesh.shape["ctx"], mesh.shape["tp"])
    return jax.shard_map(
        body,
        mesh=mesh,
        in_specs=(wide,) * 4 + (tall,) * 2,
        out_specs=(wide,) * 3 + (tall,) * 2,
        check_vma=False,
    )
```

```python
import functools

import jax
import jax.numpy as jnp
from jax import lax
from jax.experimental import pallas as pl
from jax.experimental.pallas import tpu as pltpu
from jax.sharding import PartitionSpec as P

CLIP_NORM = 512
SUB = 8
LANES = 128
MESH = pl.DeviceIdType.MESH
VMEM_BYTES = 56 * 1024 * 1024
SETTLE_BYTES = 4 * 1024 * 1024
GROUPS = 4
LAG = 2
REST = 4


def total_of(terms):
    while len(terms) > 1:
        paired = [x + y for x, y in zip(terms[::2], terms[1::2])]
        terms = paired + ([terms[-1]] if len(terms) % 2 else [])
    return terms[0]


def fused_kernel(
    n, ntp, modes, groups,
    go_in, q_in, k_in, v_in, lr_in, res_in,
    gq_ref, gk_ref, gv_ref, dres_ref, drate_ref, scale_ref,
    go_ref, q_ref, k_ref, v_ref, lr_ref, res_ref,
    p_s, g_s, ends_s, pre_s, loc_s, turn_s, lag_s, hold_s, table, fr_s, br_s,
    ea_s, mate, mate_loc, pt_s, held, ca_s, back_s, raw_s, parts, red, gath, sums, squares,
    in_sem, small_sem, pa_send, pa_recv, pl_send, pl_recv, ex_send, ex_recv, bk_send, bk_recv,
    rs_send, rs_recv, ag_send, ag_recv, fw_send, fw_recv, sq_send, sq_recv,
):
    me = lax.axis_index("ctx")
    col = lax.axis_index("tp")
    pair = me // 2
    odd = lax.rem(me, 2)
    pairs = n // 2
    plane = 2 * ntp
    here = odd * ntp + col
    rows, chans = go_ref.shape
    span = rows // SUB
    width = chans // groups
    half = width // 2
    chunks = chans // LANES
    per_group = width // LANES
    per_half = half // LANES
    pieces = 2 * modes // SUB
    own = red.shape[1]
    zero = jnp.zeros((SUB, LANES), jnp.float32)
    folds = modes // SUB

    def fetch(which, g):
        at = pl.ds(pl.multiple_of(g * width, LANES), width)
        source = (go_in, q_in, k_in, v_in)[which]
        target = (go_ref, q_ref, k_ref, v_ref)[which]
        return pltpu.make_async_copy(source.at[:, at], target.at[:, at], in_sem.at[which, g])

    rate_copy = pltpu.make_async_copy(lr_in, lr_ref, small_sem.at[0])
    residue_copy = pltpu.make_async_copy(res_in, res_ref, small_sem.at[1])
    rate_copy.start()
    for g in range(groups):
        for which in (2, 3, 0, 1):
            fetch(which, g).start()
    residue_copy.start()

    def beside(q):
        other = lax.rem(here + q, plane)
        return {"ctx": pair * 2 + other // ntp, "tp": lax.rem(other, ntp)}

    def along(k):
        return {"ctx": lax.rem(pair + k, pairs) * 2 + odd}

    across_pair = {"ctx": pair * 2 + 1 - odd}
    barrier = pltpu.get_barrier_semaphore()
    for q in range(1, plane):
        pl.semaphore_signal(barrier, inc=1, device_id=beside(q), device_id_type=MESH)
    for k in range(1, pairs):
        pl.semaphore_signal(barrier, inc=1, device_id=along(k), device_id_type=MESH)

    def wide(x, m):
        return jnp.broadcast_to(x[m : m + 1], (SUB, LANES))

    def lanes(ch):
        return pl.ds(pl.multiple_of(ch * LANES, LANES), LANES)

    def fold(f):
        return pl.ds(f * SUB, SUB)

    def turned(q, f):
        return pl.ds(f * SUB * SUB + q, SUB, stride=SUB)

    def copy_to(source, target, send, recv, place):
        return pltpu.make_async_remote_copy(
            src_ref=source, dst_ref=target, send_sem=send, recv_sem=recv, device_id=place, device_id_type=MESH
        )

    def ends(ch):
        g, c = ch // per_group, lax.rem(ch, per_group)
        at = lanes(ch)
        p_s[ch] = k_ref[:, at].astype(jnp.float32) * v_ref[:, at].astype(jnp.float32)
        g_s[ch] = go_ref[:, at].astype(jnp.float32) * q_ref[:, at].astype(jnp.float32)
        rate = jnp.exp(lr_ref[:, at])
        decay = jnp.exp(-rate)
        for first in range(0, modes, 8):
            group = range(first, min(modes, first + 8))
            a = [wide(decay, m) for m in group]
            s = [zero] * len(a)
            t = [zero] * len(a)
            for i in range(span):
                x = p_s[ch, pl.ds(i, SUB, stride=span), :]
                y = g_s[ch, pl.ds(span - 1 - i, SUB, stride=span), :]
                s = [aa * ss + x for aa, ss in zip(a, s)]
                t = [aa * tt + y for aa, tt in zip(a, t)]
            for slot, m in enumerate(group):
                ends_s[ch, 0, m * SUB : (m + 1) * SUB] = s[slot]
                ends_s[ch, 1, m * SUB : (m + 1) * SUB] = t[slot]
        far = jnp.exp(-rate * span)
        side, inner = c // per_half, lanes(lax.rem(c, per_half))
        for f in range(folds):
            step = far[f * SUB : (f + 1) * SUB]
            s = zero
            t = zero
            for q in range(SUB):
                pre_s[ch, 0, q, fold(f)] = s
                s = step * s + ends_s[ch, 0, turned(q, f)]
                pre_s[ch, 1, SUB - 1 - q, fold(f)] = t
                t = step * t + ends_s[ch, 1, turned(SUB - 1 - q, f)]
            ea_s[g, side, 0, fold(f), inner] = s
            ea_s[g, side, 1, fold(f), inner] = t

    def local(ch):
        g, c = ch // per_group, lax.rem(ch, per_group)
        side, inner = c // per_half, lanes(lax.rem(c, per_half))
        rate = jnp.exp(lr_ref[:, lanes(ch)])
        decay = jnp.exp(-rate)
        power = decay
        for k in range(1, span + 1):
            table[k * modes : (k + 1) * modes] = power * float(k)
            power = power * decay
        x = [p_s[ch, pl.ds(b, SUB, stride=span), :] for b in range(span)]
        y = [g_s[ch, pl.ds(b, SUB, stride=span), :] for b in range(span)]
        for m in range(modes):
            da, de = [], []
            for k in range(1, span + 1):
                coeff = jnp.broadcast_to(table[k * modes + m : k * modes + m + 1], (SUB, LANES))
                da.append(coeff * y[k - 1])
                if k < span:
                    de.append(coeff * x[span - 1 - k])
                if len(da) == 4:
                    da = [total_of(da)]
                if len(de) == 4:
                    de = [total_of(de)]
            turn_s[0, m * SUB : (m + 1) * SUB] = total_of(da)
            turn_s[1, m * SUB : (m + 1) * SUB] = total_of(de)
        for j in range(span):
            terms = []
            for b in range(span - j):
                terms.append(y[b + j] * x[b])
                if len(terms) == 4:
                    terms = [total_of(terms)]
            lag_s[j * SUB : (j + 1) * SUB] = total_of(terms)
        for f in range(span // SUB):
            hold_s[f * SUB : (f + 1) * SUB] = total_of([lag_s[turned(q, f)] for q in range(SUB)])
        far = jnp.exp(-rate * span)
        for f in range(folds):
            a = decay[f * SUB : (f + 1) * SUB]
            step = far[f * SUB : (f + 1) * SUB]
            v = zero
            d = zero
            for j in reversed(range(span)):
                d = a * d + v
                v = a * v + jnp.broadcast_to(hold_s[j : j + 1], (SUB, LANES))
            z = a * step * float(span)
            raw = zero
            lag = zero
            ahead = zero
            behind = zero
            for q in range(SUB):
                before = pre_s[ch, 0, q, fold(f)]
                after = pre_s[ch, 1, q, fold(f)]
                u = turn_s[0, turned(q, f)] + z * after
                w = a * turn_s[1, turned(q, f)]
                raw = raw + before * ends_s[ch, 1, turned(q, f)]
                lag = lag + before * u + after * w
                behind = step * behind + w + z * before
            for q in reversed(range(SUB)):
                u = turn_s[0, turned(q, f)] + z * pre_s[ch, 1, q, fold(f)]
                ahead = step * ahead + u
            loc_s[g, side, 0, fold(f), inner] = v + a * raw
            loc_s[g, side, 1, fold(f), inner] = a * d + lag
            loc_s[g, side, 2, fold(f), inner] = ahead
            loc_s[g, side, 3, fold(f), inner] = behind

    def couple(g):
        return copy_to(ea_s.at[g, 1 - odd], mate.at[g], pa_send.at[g], pa_recv.at[g], across_pair)

    def pool(g):
        return copy_to(loc_s.at[g, 1 - odd], mate_loc.at[g], pl_send.at[g], pl_recv.at[g], across_pair)

    def exchange(g, k):
        there = lax.rem(pair + k, pairs)
        which = jnp.where(there < pair, 1, 0)
        return copy_to(
            pt_s.at[g, which], held.at[g, k - 1], ex_send.at[g, k - 1], ex_recv.at[g, k - 1], along(k)
        )

    def hand(g):
        return copy_to(back_s.at[g], ca_s.at[g, odd], bk_send.at[g], bk_recv.at[g], across_pair)

    def scatter(g, k):
        there = lax.rem(pair + k, pairs)
        return copy_to(
            raw_s.at[g, pl.ds(there * own, own)],
            parts.at[g, k - 1], rs_send.at[g, k - 1], rs_recv.at[g, k - 1], along(k),
        )

    def gather(g, k):
        return copy_to(red.at[g], gath.at[g, odd, pair], ag_send.at[g, k - 1], ag_recv.at[g, k - 1], along(k))

    def forward(g):
        return copy_to(gath.at[g, odd], gath.at[g, odd], fw_send.at[g], fw_recv.at[g], across_pair)

    def norm(q):
        return copy_to(squares.at[here], squares.at[here], sq_send.at[q - 1], sq_recv.at[q - 1], beside(q))

    def rates(g):
        at = pl.ds(pl.multiple_of(g * width + odd * half, LANES), half)
        return jnp.exp(lr_ref[:, at])

    def ordered(g):
        mine, other = ea_s[g, odd], mate[g]
        return jnp.where(odd == 1, other, mine), jnp.where(odd == 1, mine, other)

    def join(g):
        couple(g).wait_recv()
        across = jnp.exp(-rates(g) * rows)
        early, late = ordered(g)
        pt_s[g, 0] = across * early[0] + late[0]
        pt_s[g, 1] = early[1] + across * late[1]
        for k in range(1, pairs):
            exchange(g, k).start()

    def carry(g):
        rate = rates(g)
        back_s[g] = jnp.zeros_like(back_s[g])
        for k in range(1, pairs):
            exchange(g, k).wait_recv()
            origin = lax.rem(pair - k + pairs, pairs)
            which = jnp.where(origin < pair, 0, 1)
            gap = jnp.where(origin < pair, pair - origin, origin - pair) - 1
            power = jnp.exp(-rate * (gap * (2 * rows)).astype(jnp.float32))
            back_s[g, which] += power * held[g, k - 1]
        across = jnp.exp(-rate * rows)
        early, late = ordered(g)
        from_past = back_s[g, 0]
        from_next = back_s[g, 1]
        past = from_past, early[0] + across * from_past
        ahead = late[1] + across * from_next, from_next
        ca_s[g, odd, 0] = jnp.where(odd == 1, past[1], past[0])
        ca_s[g, odd, 1] = jnp.where(odd == 1, ahead[1], ahead[0])
        back_s[g, 0] = jnp.where(odd == 1, past[0], past[1])
        back_s[g, 1] = jnp.where(odd == 1, ahead[0], ahead[1])
        hand(g).start()

    def grads(g, c):
        inner = lanes(c)
        at = pl.ds(pl.multiple_of(g * width + odd * half + c * LANES, LANES), LANES)
        rate = jnp.exp(lr_ref[:, at])
        decay = jnp.exp(-rate)
        root = jnp.sqrt(2.0 * rate)
        weight = res_ref[:, at] * root
        through = jnp.exp(-rate * (rows + 1)) * float(rows)
        raw, lag = [], []
        for loc, past, ahead, first in (
            (loc_s.at[g, odd], ca_s[g, odd, 0, :, inner], ca_s[g, odd, 1, :, inner], ea_s[g, odd, 1, :, inner]),
            (mate_loc.at[g], back_s[g, 0, :, inner], back_s[g, 1, :, inner], mate[g, 1, :, inner]),
        ):
            raw.append(loc[0, :, inner] + decay * (past * first))
            lag.append(
                loc[1, :, inner] + past * loc[2, :, inner] + ahead * (loc[3, :, inner] + through * past)
            )
        raw_weight = raw[0] + raw[1]
        both = (root * raw_weight, weight * (0.5 * raw_weight - rate * (lag[0] + lag[1])))
        for piece in range(pieces):
            low = piece % (pieces // 2) * SUB
            raw_s[g, c * pieces + piece] = both[piece // (pieces // 2)][low : low + SUB]

    def reduce_start(g):
        carry(g)
        pool(g).wait_recv()
        for c in range(per_half):
            grads(g, c)
        for k in range(1, pairs):
            scatter(g, k).start()

    def reduce_finish(g):
        mine = raw_s[g, pl.ds(pair * own, own)]
        for k in range(1, pairs):
            scatter(g, k).wait_recv()
            mine = mine + parts[g, k - 1]
        red[g] = mine
        for k in range(1, pairs):
            gather(g, k).start()
        gath[g, odd, pair] = mine

    def unpack(g, side):
        for c in range(per_half):
            at = pl.ds(pl.multiple_of(g * width + side * half + c * LANES, LANES), LANES)
            for piece in range(pieces):
                tile = c * pieces + piece
                low = piece % (pieces // 2) * SUB
                ref = dres_ref if piece < pieces // 2 else drate_ref
                ref[low : low + SUB, at] = gath[g, side, tile // own, tile % own]

    def pass_on(g):
        for k in range(1, pairs):
            gather(g, k).wait_recv()
        forward(g).start()
        whole = gath[g, odd]
        sums[...] += jnp.sum(jnp.sum(whole * whole, axis=0), axis=0)
        unpack(g, odd)

    def filters(ch):
        g, c = ch // per_group, lax.rem(ch, per_group)
        side, inner = c // per_half, lanes(lax.rem(c, per_half))
        at = lanes(ch)
        rate = jnp.exp(lr_ref[:, at])
        decay = jnp.exp(-rate)
        far = jnp.exp(-rate * span)
        for f in range(folds):
            step = far[f * SUB : (f + 1) * SUB]
            past = ca_s[g, side, 0, fold(f), inner]
            ahead = ca_s[g, side, 1, fold(f), inner]
            for q in range(SUB):
                turn_s[0, turned(q, f)] = pre_s[ch, 0, q, fold(f)] + past
                turn_s[1, turned(SUB - 1 - q, f)] = pre_s[ch, 1, SUB - 1 - q, fold(f)] + ahead
                past = step * past
                ahead = step * ahead
        power = res_ref[:, at] * jnp.sqrt(2.0 * rate)
        for k in range(span + 1):
            table[k * modes : (k + 1) * modes] = power
            power = power * decay
        for f in range(span // SUB):
            hold_s[f * SUB : (f + 1) * SUB] = total_of(
                [table[pl.ds(f * SUB * modes + m, SUB, stride=modes)] for m in range(modes)]
            )
        h = [jnp.broadcast_to(hold_s[j : j + 1], (SUB, LANES)) for j in range(span)]
        x = [p_s[ch, pl.ds(b, SUB, stride=span), :] for b in range(span)]
        for b in range(span):
            terms = []
            for j in range(b + 1):
                terms.append(h[j] * x[b - j])
                if len(terms) == 4:
                    terms = [total_of(terms)]
            lag_s[b * SUB : (b + 1) * SUB] = total_of(terms)
        y = [g_s[ch, pl.ds(b, SUB, stride=span), :] for b in range(span)]
        for b in range(span):
            terms = []
            for j in range(span - b):
                terms.append(h[j] * y[b + j])
                if len(terms) == 4:
                    terms = [total_of(terms)]
            lag_s[(span + b) * SUB : (span + b + 1) * SUB] = total_of(terms)
        s = [turn_s[0, m * SUB : (m + 1) * SUB] for m in range(modes)]
        t = [turn_s[1, m * SUB : (m + 1) * SUB] for m in range(modes)]
        for k in range(1, span + 1):
            b = k - 1
            r = span - k
            fore = [lag_s[b * SUB : (b + 1) * SUB]]
            back = [lag_s[(span + r) * SUB : (span + r + 1) * SUB]]
            for m in range(modes):
                coeff = jnp.broadcast_to(table[k * modes + m : k * modes + m + 1], (SUB, LANES))
                fore.append(coeff * s[m])
                back.append(coeff * t[m])
                if len(fore) == 4:
                    fore = [total_of(fore)]
                    back = [total_of(back)]
            fr_s[pl.ds(b, SUB, stride=span), :] = total_of(fore)
            br_s[pl.ds(r, SUB, stride=span), :] = total_of(back)
        gq_ref[:, at] = (go_ref[:, at].astype(jnp.float32) * fr_s[...]).astype(gq_ref.dtype)
        back = br_s[...]
        gk_ref[:, at] = (back * v_ref[:, at].astype(jnp.float32)).astype(gk_ref.dtype)
        gv_ref[:, at] = (back * k_ref[:, at].astype(jnp.float32)).astype(gv_ref.dtype)

    if raw_s.shape[1] > per_half * pieces:
        raw_s[...] = jnp.zeros_like(raw_s)

    def part(g, theirs, c):
        return g * per_group + jnp.where(theirs, 1 - odd, odd) * per_half + c

    def each(act, g, theirs):
        def one(c, _):
            act(part(g, theirs, c))
            return 0

        lax.fori_loop(0, per_half, one, 0)

    def first_stage(g, _):
        for which in range(4):
            fetch(which, g).wait()
        each(ends, g, True)

        @pl.when(g == 0)
        def _():
            pl.semaphore_wait(barrier, plane + pairs - 2)

        couple(g).start()
        return 0

    def second_stage(g, _):
        each(local, g, True)
        pool(g).start()
        each(ends, g, False)
        join(g)
        return 0

    def start_at(h):
        return h + min(LAG, groups - 1)

    def finish_at(h):
        return min(start_at(h) + REST, 3 * groups - 1)

    def drain(g, _):
        couple(g).wait_send()
        pool(g).wait_send()
        hand(g).wait_send()
        for k in range(1, pairs):
            exchange(g, k).wait_send()
            scatter(g, k).wait_send()
            gather(g, k).wait_send()
        return 0

    def pass_at(h):
        return max(min(finish_at(h) + REST, 3 * groups - 1), groups)

    def third_stage(g, _):
        each(local, g, False)
        for h in range(groups):
            if start_at(h) < groups:
                pl.when(g == start_at(h))(functools.partial(reduce_start, h))
        return 0

    def fourth_stage(i, _):
        theirs = i // groups == 1
        g = lax.rem(i, groups)

        @pl.when(theirs)
        def _():
            hand(g).wait_recv()

        each(filters, g, theirs)
        for h in range(groups):
            if start_at(h) >= groups:
                pl.when(i == start_at(h) - groups)(functools.partial(reduce_start, h))
        for h in range(groups):
            pl.when(i == max(finish_at(h) - groups, 0))(functools.partial(reduce_finish, h))
        for h in range(groups):
            pl.when(i == pass_at(h) - groups)(functools.partial(pass_on, h))
        return 0

    sums[...] = zero
    rate_copy.wait()
    lax.fori_loop(0, groups, first_stage, 0)
    lax.fori_loop(0, groups, second_stage, 0)
    residue_copy.wait()
    lax.fori_loop(0, groups, third_stage, 0)
    lax.fori_loop(0, 2 * groups, fourth_stage, 0)
    squares[here] = sums[...]
    for q in range(1, plane):
        norm(q).start()
    lax.fori_loop(0, groups, drain, 0)
    for g in range(groups):
        forward(g).wait_recv()
        unpack(g, 1 - odd)
    for q in range(1, plane):
        norm(q).wait()
    square = jnp.sum(jnp.sum(squares[...], axis=0), keepdims=True)
    scale = jnp.minimum(1.0, CLIP_NORM / jnp.sqrt(square + 1e-06))
    scale_ref[...] = jnp.broadcast_to(scale, scale_ref.shape)
    for g in range(groups):
        forward(g).wait_send()


def settle_kernel(
    gq_in, gk_in, gv_in, dres_in, drate_in, scale_in,
    gq_ref, gk_ref, gv_ref, dres_ref, drate_ref, scaled, sem,
):
    copies = [
        pltpu.make_async_copy(source, target, sem.at[i])
        for i, (source, target) in enumerate(
            ((gq_in, gq_ref), (gk_in, gk_ref), (gv_in, gv_ref), (scaled.at[0], dres_ref), (scaled.at[1], drate_ref))
        )
    ]
    for copy in copies[:3]:
        copy.start()
    scaled[0] = dres_in[...] * scale_in[...]
    copies[3].start()
    scaled[1] = drate_in[...] * scale_in[...]
    copies[4].start()
    for copy in copies:
        copy.wait()


def per_device(n, ntp, grad_out, query_in, key_in, value_in, residue, log_rate):
    rows, chans = grad_out.shape
    modes = residue.shape[1]
    span = rows // SUB
    chunks = chans // LANES
    pairs = n // 2
    groups = GROUPS if chunks % (2 * GROUPS) == 0 and n <= 32 else 1
    width = chans // groups
    half = width // 2
    own = -(-(half // LANES * 2 * modes // SUB) // pairs)
    f32 = jnp.float32
    shape = jax.ShapeDtypeStruct
    hbm = pl.BlockSpec(memory_space=pltpu.HBM)
    vmem = pl.BlockSpec(memory_space=pltpu.VMEM)
    buffer = lambda *dims: pltpu.VMEM(dims, f32)
    tile = lambda *lead: pltpu.VMEM((*lead, SUB, LANES), f32)
    flags = lambda *dims: pltpu.SemaphoreType.DMA(dims)
    wide_out = pltpu.VMEM((rows, chans), grad_out.dtype)
    results = pl.pallas_call(
        functools.partial(fused_kernel, n, ntp, modes, groups),
        out_shape=(wide_out,) * 3 + (pltpu.VMEM((modes, chans), f32),) * 3,
        in_specs=[hbm] * 6,
        out_specs=(vmem,) * 6,
        scratch_shapes=[
            *[pltpu.VMEM((rows, chans), grad_out.dtype)] * 4,
            buffer(modes, chans),
            buffer(modes, chans),
            buffer(chunks, rows, LANES),
            buffer(chunks, rows, LANES),
            buffer(chunks, 2, modes * SUB, LANES),
            buffer(chunks, 2, SUB, modes, LANES),
            buffer(groups, 2, 4, modes, half),
            buffer(2, modes * SUB, LANES),
            buffer(2 * span * SUB, LANES),
            buffer(span, LANES),
            buffer((span + 1) * modes, LANES),
            buffer(rows, LANES),
            buffer(rows, LANES),
            buffer(groups, 2, 2, modes, half),
            buffer(groups, 2, modes, half),
            buffer(groups, 4, modes, half),
            buffer(groups, 2, modes, half),
            buffer(groups, pairs - 1, modes, half),
            buffer(groups, 2, 2, modes, half),
            buffer(groups, 2, modes, half),
            tile(groups, own * pairs),
            tile(groups, pairs - 1, own),
            tile(groups, own),
            tile(groups, 2, pairs, own),
            tile(),
            tile(2 * ntp),
            flags(4, groups), flags(2),
            flags(groups), flags(groups),
            flags(groups), flags(groups),
            flags(groups, pairs - 1), flags(groups, pairs - 1),
            flags(groups), flags(groups),
            flags(groups, pairs - 1), flags(groups, pairs - 1),
            flags(groups, pairs - 1), flags(groups, pairs - 1),
            flags(groups), flags(groups),
            flags(2 * ntp - 1), flags(2 * ntp - 1),
        ],
        compiler_params=pltpu.CompilerParams(
            collective_id=0, has_side_effects=True, vmem_limit_bytes=VMEM_BYTES
        ),
        name="fused",
    )(grad_out, query_in, key_in, value_in, log_rate.T, residue.T)
    anywhere = pl.BlockSpec(memory_space=pl.ANY)
    wide, tall = shape((rows, chans), grad_out.dtype), shape((modes, chans), f32)
    grad_query, grad_key, grad_value, d_res, d_rate = pl.pallas_call(
        settle_kernel,
        out_shape=(wide,) * 3 + (tall,) * 2,
        in_specs=[anywhere] * 3 + [vmem] * 3,
        out_specs=(anywhere,) * 5,
        scratch_shapes=[buffer(2, modes, chans), flags(5)],
        compiler_params=pltpu.CompilerParams(vmem_limit_bytes=SETTLE_BYTES),
        name="settle",
    )(*results)
    return grad_query, grad_key, grad_value, d_res.T, d_rate.T


def solution(mesh):
    wide = P("ctx", "tp")
    tall = P("tp", None)
    body = functools.partial(per_device, mesh.shape["ctx"], mesh.shape["tp"])
    return jax.shard_map(
        body,
        mesh=mesh,
        in_specs=(wide,) * 4 + (tall,) * 2,
        out_specs=(wide,) * 3 + (tall,) * 2,
        check_vma=False,
    )
```

```python
import functools

import jax
import jax.numpy as jnp
from jax import lax
from jax.experimental import pallas as pl
from jax.experimental.pallas import tpu as pltpu
from jax.sharding import PartitionSpec as P

CLIP_NORM = 512
SUB = 8
LANES = 128
MESH = pl.DeviceIdType.MESH
VMEM_BYTES = 56 * 1024 * 1024
SETTLE_BYTES = 4 * 1024 * 1024
GROUPS = 4
STARTS = (3, 4)
FINISHES = (8, 8)
PASSES = (11, 11)


def total_of(terms):
    while len(terms) > 1:
        paired = [x + y for x, y in zip(terms[::2], terms[1::2])]
        terms = paired + ([terms[-1]] if len(terms) % 2 else [])
    return terms[0]


def fused_kernel(
    n, ntp, modes, groups,
    go_in, q_in, k_in, v_in, lr_in, res_in,
    gq_ref, gk_ref, gv_ref, dres_ref, drate_ref, scale_ref,
    go_ref, q_ref, k_ref, v_ref, lr_ref, res_ref,
    p_s, g_s, ends_s, pre_s, loc_s, turn_s, lag_s, hold_s, table, fr_s, br_s,
    ea_s, mate, mate_loc, pt_s, held, ca_s, back_s, raw_s, parts, red, gath, sums, squares,
    in_sem, small_sem, pa_send, pa_recv, pl_send, pl_recv, ex_send, ex_recv, bk_send, bk_recv,
    rs_send, rs_recv, ag_send, ag_recv, fw_send, fw_recv, sq_send, sq_recv,
):
    me = lax.axis_index("ctx")
    col = lax.axis_index("tp")
    pair = me // 2
    odd = lax.rem(me, 2)
    pairs = n // 2
    plane = 2 * ntp
    here = odd * ntp + col
    rows, chans = go_ref.shape
    span = rows // SUB
    width = chans // groups
    half = width // 2
    chunks = chans // LANES
    per_group = width // LANES
    per_half = half // LANES
    pieces = 2 * modes // SUB
    own = red.shape[1]
    batch = 2 if groups % 2 == 0 else 1
    batches = groups // batch
    zero = jnp.zeros((SUB, LANES), jnp.float32)
    folds = modes // SUB

    def fetch(which, g):
        at = pl.ds(pl.multiple_of(g * width, LANES), width)
        source = (go_in, q_in, k_in, v_in)[which]
        target = (go_ref, q_ref, k_ref, v_ref)[which]
        return pltpu.make_async_copy(source.at[:, at], target.at[:, at], in_sem.at[which, g])

    rate_copy = pltpu.make_async_copy(lr_in, lr_ref, small_sem.at[0])
    residue_copy = pltpu.make_async_copy(res_in, res_ref, small_sem.at[1])
    rate_copy.start()
    for g in range(groups):
        for which in (2, 3, 0, 1):
            fetch(which, g).start()
    residue_copy.start()

    def beside(q):
        other = lax.rem(here + q, plane)
        return {"ctx": pair * 2 + other // ntp, "tp": lax.rem(other, ntp)}

    def along(k):
        return {"ctx": lax.rem(pair + k, pairs) * 2 + odd}

    across_pair = {"ctx": pair * 2 + 1 - odd}
    barrier = pltpu.get_barrier_semaphore()
    for q in range(1, plane):
        pl.semaphore_signal(barrier, inc=1, device_id=beside(q), device_id_type=MESH)
    for k in range(1, pairs):
        pl.semaphore_signal(barrier, inc=1, device_id=along(k), device_id_type=MESH)

    def wide(x, m):
        return jnp.broadcast_to(x[m : m + 1], (SUB, LANES))

    def lanes(ch):
        return pl.ds(pl.multiple_of(ch * LANES, LANES), LANES)

    def fold(f):
        return pl.ds(f * SUB, SUB)

    def turned(q, f):
        return pl.ds(f * SUB * SUB + q, SUB, stride=SUB)

    def copy_to(source, target, send, recv, place):
        return pltpu.make_async_remote_copy(
            src_ref=source, dst_ref=target, send_sem=send, recv_sem=recv, device_id=place, device_id_type=MESH
        )

    def ends(ch):
        g, c = ch // per_group, lax.rem(ch, per_group)
        at = lanes(ch)
        p_s[ch] = k_ref[:, at].astype(jnp.float32) * v_ref[:, at].astype(jnp.float32)
        g_s[ch] = go_ref[:, at].astype(jnp.float32) * q_ref[:, at].astype(jnp.float32)
        rate = jnp.exp(lr_ref[:, at])
        decay = jnp.exp(-rate)
        for first in range(0, modes, 8):
            group = range(first, min(modes, first + 8))
            a = [wide(decay, m) for m in group]
            s = [zero] * len(a)
            t = [zero] * len(a)
            for i in range(span):
                x = p_s[ch, pl.ds(i, SUB, stride=span), :]
                y = g_s[ch, pl.ds(span - 1 - i, SUB, stride=span), :]
                s = [aa * ss + x for aa, ss in zip(a, s)]
                t = [aa * tt + y for aa, tt in zip(a, t)]
            for slot, m in enumerate(group):
                ends_s[ch, 0, m * SUB : (m + 1) * SUB] = s[slot]
                ends_s[ch, 1, m * SUB : (m + 1) * SUB] = t[slot]
        far = jnp.exp(-rate * span)
        side, inner = c // per_half, lanes(lax.rem(c, per_half))
        for f in range(folds):
            step = far[f * SUB : (f + 1) * SUB]
            s = zero
            t = zero
            for q in range(SUB):
                pre_s[ch, 0, q, fold(f)] = s
                s = step * s + ends_s[ch, 0, turned(q, f)]
                pre_s[ch, 1, SUB - 1 - q, fold(f)] = t
                t = step * t + ends_s[ch, 1, turned(SUB - 1 - q, f)]
            ea_s[g, side, 0, fold(f), inner] = s
            ea_s[g, side, 1, fold(f), inner] = t

    def local(ch):
        g, c = ch // per_group, lax.rem(ch, per_group)
        side, inner = c // per_half, lanes(lax.rem(c, per_half))
        rate = jnp.exp(lr_ref[:, lanes(ch)])
        decay = jnp.exp(-rate)
        power = decay
        for k in range(1, span + 1):
            table[k * modes : (k + 1) * modes] = power * float(k)
            power = power * decay
        x = [p_s[ch, pl.ds(b, SUB, stride=span), :] for b in range(span)]
        y = [g_s[ch, pl.ds(b, SUB, stride=span), :] for b in range(span)]
        for m in range(modes):
            da, de = [], []
            for k in range(1, span + 1):
                coeff = jnp.broadcast_to(table[k * modes + m : k * modes + m + 1], (SUB, LANES))
                da.append(coeff * y[k - 1])
                if k < span:
                    de.append(coeff * x[span - 1 - k])
                if len(da) == 4:
                    da = [total_of(da)]
                if len(de) == 4:
                    de = [total_of(de)]
            turn_s[0, m * SUB : (m + 1) * SUB] = total_of(da)
            turn_s[1, m * SUB : (m + 1) * SUB] = total_of(de)
        for j in range(span):
            terms = []
            for b in range(span - j):
                terms.append(y[b + j] * x[b])
                if len(terms) == 4:
                    terms = [total_of(terms)]
            lag_s[j * SUB : (j + 1) * SUB] = total_of(terms)
        for f in range(span // SUB):
            hold_s[f * SUB : (f + 1) * SUB] = total_of([lag_s[turned(q, f)] for q in range(SUB)])
        far = jnp.exp(-rate * span)
        for f in range(folds):
            a = decay[f * SUB : (f + 1) * SUB]
            step = far[f * SUB : (f + 1) * SUB]
            v = zero
            d = zero
            for j in reversed(range(span)):
                d = a * d + v
                v = a * v + jnp.broadcast_to(hold_s[j : j + 1], (SUB, LANES))
            z = a * step * float(span)
            raw = zero
            lag = zero
            ahead = zero
            behind = zero
            for q in range(SUB):
                before = pre_s[ch, 0, q, fold(f)]
                after = pre_s[ch, 1, q, fold(f)]
                u = turn_s[0, turned(q, f)] + z * after
                w = a * turn_s[1, turned(q, f)]
                raw = raw + before * ends_s[ch, 1, turned(q, f)]
                lag = lag + before * u + after * w
                behind = step * behind + w + z * before
            for q in reversed(range(SUB)):
                u = turn_s[0, turned(q, f)] + z * pre_s[ch, 1, q, fold(f)]
                ahead = step * ahead + u
            loc_s[g, side, 0, fold(f), inner] = v + a * raw
            loc_s[g, side, 1, fold(f), inner] = a * d + lag
            loc_s[g, side, 2, fold(f), inner] = ahead
            loc_s[g, side, 3, fold(f), inner] = behind

    def couple(g):
        return copy_to(ea_s.at[g, 1 - odd], mate.at[g], pa_send.at[g], pa_recv.at[g], across_pair)

    def pool(g):
        return copy_to(loc_s.at[g, 1 - odd], mate_loc.at[g], pl_send.at[g], pl_recv.at[g], across_pair)

    def exchange(g, k):
        there = lax.rem(pair + k, pairs)
        which = jnp.where(there < pair, 1, 0)
        return copy_to(
            pt_s.at[g, which], held.at[g, k - 1], ex_send.at[g, k - 1], ex_recv.at[g, k - 1], along(k)
        )

    def hand(g):
        return copy_to(back_s.at[g], ca_s.at[g, odd], bk_send.at[g], bk_recv.at[g], across_pair)

    def batched(b):
        return pl.ds(b * batch, batch)

    def scatter(b, k):
        there = lax.rem(pair + k, pairs)
        return copy_to(
            raw_s.at[batched(b), pl.ds(there * own, own)],
            parts.at[batched(b), k - 1], rs_send.at[b, k - 1], rs_recv.at[b, k - 1], along(k),
        )

    def gather(b, k):
        return copy_to(
            red.at[batched(b)], gath.at[batched(b), odd, pair], ag_send.at[b, k - 1], ag_recv.at[b, k - 1], along(k)
        )

    def forward(b):
        mine = gath.at[batched(b), odd]
        return copy_to(mine, mine, fw_send.at[b], fw_recv.at[b], across_pair)

    def norm(q):
        return copy_to(squares.at[here], squares.at[here], sq_send.at[q - 1], sq_recv.at[q - 1], beside(q))

    def rates(g):
        at = pl.ds(pl.multiple_of(g * width + odd * half, LANES), half)
        return jnp.exp(lr_ref[:, at])

    def ordered(g):
        mine, other = ea_s[g, odd], mate[g]
        return jnp.where(odd == 1, other, mine), jnp.where(odd == 1, mine, other)

    def join(g):
        couple(g).wait_recv()
        across = jnp.exp(-rates(g) * rows)
        early, late = ordered(g)
        pt_s[g, 0] = across * early[0] + late[0]
        pt_s[g, 1] = early[1] + across * late[1]
        for k in range(1, pairs):
            exchange(g, k).start()

    def carry(g):
        rate = rates(g)
        back_s[g] = jnp.zeros_like(back_s[g])
        for k in range(1, pairs):
            exchange(g, k).wait_recv()
            origin = lax.rem(pair - k + pairs, pairs)
            which = jnp.where(origin < pair, 0, 1)
            gap = jnp.where(origin < pair, pair - origin, origin - pair) - 1
            power = jnp.exp(-rate * (gap * (2 * rows)).astype(jnp.float32))
            back_s[g, which] += power * held[g, k - 1]
        across = jnp.exp(-rate * rows)
        early, late = ordered(g)
        from_past = back_s[g, 0]
        from_next = back_s[g, 1]
        past = from_past, early[0] + across * from_past
        ahead = late[1] + across * from_next, from_next
        ca_s[g, odd, 0] = jnp.where(odd == 1, past[1], past[0])
        ca_s[g, odd, 1] = jnp.where(odd == 1, ahead[1], ahead[0])
        back_s[g, 0] = jnp.where(odd == 1, past[0], past[1])
        back_s[g, 1] = jnp.where(odd == 1, ahead[0], ahead[1])
        hand(g).start()

    def grads(g, c):
        inner = lanes(c)
        at = pl.ds(pl.multiple_of(g * width + odd * half + c * LANES, LANES), LANES)
        rate = jnp.exp(lr_ref[:, at])
        decay = jnp.exp(-rate)
        root = jnp.sqrt(2.0 * rate)
        weight = res_ref[:, at] * root
        through = jnp.exp(-rate * (rows + 1)) * float(rows)
        raw, lag = [], []
        for loc, past, ahead, first in (
            (loc_s.at[g, odd], ca_s[g, odd, 0, :, inner], ca_s[g, odd, 1, :, inner], ea_s[g, odd, 1, :, inner]),
            (mate_loc.at[g], back_s[g, 0, :, inner], back_s[g, 1, :, inner], mate[g, 1, :, inner]),
        ):
            raw.append(loc[0, :, inner] + decay * (past * first))
            lag.append(
                loc[1, :, inner] + past * loc[2, :, inner] + ahead * (loc[3, :, inner] + through * past)
            )
        raw_weight = raw[0] + raw[1]
        both = (root * raw_weight, weight * (0.5 * raw_weight - rate * (lag[0] + lag[1])))
        for piece in range(pieces):
            low = piece % (pieces // 2) * SUB
            raw_s[g, c * pieces + piece] = both[piece // (pieces // 2)][low : low + SUB]

    def reduce_start(b):
        for g in range(b * batch, (b + 1) * batch):
            carry(g)
            pool(g).wait_recv()
            for c in range(per_half):
                grads(g, c)
        for k in range(1, pairs):
            scatter(b, k).start()

    def reduce_finish(b):
        mine = raw_s[batched(b), pl.ds(pair * own, own)]
        for k in range(1, pairs):
            scatter(b, k).wait_recv()
            mine = mine + parts[batched(b), k - 1]
        red[batched(b)] = mine
        for k in range(1, pairs):
            gather(b, k).start()
        gath[batched(b), odd, pair] = mine

    def unpack(g, side):
        for c in range(per_half):
            at = pl.ds(pl.multiple_of(g * width + side * half + c * LANES, LANES), LANES)
            for piece in range(pieces):
                tile = c * pieces + piece
                low = piece % (pieces // 2) * SUB
                ref = dres_ref if piece < pieces // 2 else drate_ref
                ref[low : low + SUB, at] = gath[g, side, tile // own, tile % own]

    def pass_on(b):
        for k in range(1, pairs):
            gather(b, k).wait_recv()
        forward(b).start()
        for g in range(b * batch, (b + 1) * batch):
            whole = gath[g, odd]
            sums[...] += jnp.sum(jnp.sum(whole * whole, axis=0), axis=0)

    def filters(ch):
        g, c = ch // per_group, lax.rem(ch, per_group)
        side, inner = c // per_half, lanes(lax.rem(c, per_half))
        at = lanes(ch)
        rate = jnp.exp(lr_ref[:, at])
        decay = jnp.exp(-rate)
        far = jnp.exp(-rate * span)
        for f in range(folds):
            step = far[f * SUB : (f + 1) * SUB]
            past = ca_s[g, side, 0, fold(f), inner]
            ahead = ca_s[g, side, 1, fold(f), inner]
            for q in range(SUB):
                turn_s[0, turned(q, f)] = pre_s[ch, 0, q, fold(f)] + past
                turn_s[1, turned(SUB - 1 - q, f)] = pre_s[ch, 1, SUB - 1 - q, fold(f)] + ahead
                past = step * past
                ahead = step * ahead
        power = res_ref[:, at] * jnp.sqrt(2.0 * rate)
        for k in range(span + 1):
            table[k * modes : (k + 1) * modes] = power
            power = power * decay
        for f in range(span // SUB):
            hold_s[f * SUB : (f + 1) * SUB] = total_of(
                [table[pl.ds(f * SUB * modes + m, SUB, stride=modes)] for m in range(modes)]
            )
        h = [jnp.broadcast_to(hold_s[j : j + 1], (SUB, LANES)) for j in range(span)]
        x = [p_s[ch, pl.ds(b, SUB, stride=span), :] for b in range(span)]
        for b in range(span):
            terms = []
            for j in range(b + 1):
                terms.append(h[j] * x[b - j])
                if len(terms) == 4:
                    terms = [total_of(terms)]
            lag_s[b * SUB : (b + 1) * SUB] = total_of(terms)
        y = [g_s[ch, pl.ds(b, SUB, stride=span), :] for b in range(span)]
        for b in range(span):
            terms = []
            for j in range(span - b):
                terms.append(h[j] * y[b + j])
                if len(terms) == 4:
                    terms = [total_of(terms)]
            lag_s[(span + b) * SUB : (span + b + 1) * SUB] = total_of(terms)
        s = [turn_s[0, m * SUB : (m + 1) * SUB] for m in range(modes)]
        t = [turn_s[1, m * SUB : (m + 1) * SUB] for m in range(modes)]
        for k in range(1, span + 1):
            b = k - 1
            r = span - k
            fore = [lag_s[b * SUB : (b + 1) * SUB]]
            back = [lag_s[(span + r) * SUB : (span + r + 1) * SUB]]
            for m in range(modes):
                coeff = jnp.broadcast_to(table[k * modes + m : k * modes + m + 1], (SUB, LANES))
                fore.append(coeff * s[m])
                back.append(coeff * t[m])
                if len(fore) == 4:
                    fore = [total_of(fore)]
                    back = [total_of(back)]
            fr_s[pl.ds(b, SUB, stride=span), :] = total_of(fore)
            br_s[pl.ds(r, SUB, stride=span), :] = total_of(back)
        gq_ref[:, at] = (go_ref[:, at].astype(jnp.float32) * fr_s[...]).astype(gq_ref.dtype)
        back = br_s[...]
        gk_ref[:, at] = (back * v_ref[:, at].astype(jnp.float32)).astype(gk_ref.dtype)
        gv_ref[:, at] = (back * k_ref[:, at].astype(jnp.float32)).astype(gv_ref.dtype)

    if raw_s.shape[1] > per_half * pieces:
        raw_s[...] = jnp.zeros_like(raw_s)

    def part(g, theirs, c):
        return g * per_group + jnp.where(theirs, 1 - odd, odd) * per_half + c

    def each(act, g, theirs):
        def one(c, _):
            act(part(g, theirs, c))
            return 0

        lax.fori_loop(0, per_half, one, 0)

    def first_stage(g, _):
        for which in range(4):
            fetch(which, g).wait()
        each(ends, g, True)

        @pl.when(g == 0)
        def _():
            pl.semaphore_wait(barrier, plane + pairs - 2)

        couple(g).start()
        return 0

    def second_stage(g, _):
        each(local, g, True)
        pool(g).start()
        each(ends, g, False)
        join(g)
        return 0

    def start_at(b):
        return STARTS[b] if batches > 1 else 0

    def finish_at(b):
        return FINISHES[b] if batches > 1 else 1

    def drain(g, _):
        couple(g).wait_send()
        pool(g).wait_send()
        hand(g).wait_send()
        for k in range(1, pairs):
            exchange(g, k).wait_send()
        return 0

    def pass_at(b):
        return PASSES[b] if batches > 1 else 2

    def third_stage(g, _):
        each(local, g, False)
        for h in range(batches):
            if start_at(h) < groups:
                pl.when(g == start_at(h))(functools.partial(reduce_start, h))
        return 0

    def fourth_stage(i, _):
        theirs = i // groups == 1
        g = lax.rem(i, groups)

        @pl.when(theirs)
        def _():
            hand(g).wait_recv()

        each(filters, g, theirs)
        for h in range(batches):
            if start_at(h) >= groups:
                pl.when(i == start_at(h) - groups)(functools.partial(reduce_start, h))
        for h in range(batches):
            pl.when(i == max(finish_at(h) - groups, 0))(functools.partial(reduce_finish, h))
        for h in range(batches):
            pl.when(i == pass_at(h) - groups)(functools.partial(pass_on, h))
        return 0

    sums[...] = zero
    rate_copy.wait()
    lax.fori_loop(0, groups, first_stage, 0)
    lax.fori_loop(0, groups, second_stage, 0)
    residue_copy.wait()
    lax.fori_loop(0, groups, third_stage, 0)
    lax.fori_loop(0, 2 * groups, fourth_stage, 0)
    squares[here] = sums[...]
    for q in range(1, plane):
        norm(q).start()
    for g in range(groups):
        unpack(g, odd)
    lax.fori_loop(0, groups, drain, 0)
    for b in range(batches):
        for k in range(1, pairs):
            scatter(b, k).wait_send()
            gather(b, k).wait_send()
    for b in range(batches):
        forward(b).wait_recv()
        for g in range(b * batch, (b + 1) * batch):
            unpack(g, 1 - odd)
    for q in range(1, plane):
        norm(q).wait()
    square = jnp.sum(jnp.sum(squares[...], axis=0), keepdims=True)
    scale = jnp.minimum(1.0, CLIP_NORM / jnp.sqrt(square + 1e-06))
    scale_ref[...] = jnp.broadcast_to(scale, scale_ref.shape)
    for b in range(batches):
        forward(b).wait_send()


def settle_kernel(
    gq_in, gk_in, gv_in, dres_in, drate_in, scale_in,
    gq_ref, gk_ref, gv_ref, dres_ref, drate_ref, scaled, sem,
):
    copies = [
        pltpu.make_async_copy(source, target, sem.at[i])
        for i, (source, target) in enumerate(
            ((gq_in, gq_ref), (gk_in, gk_ref), (gv_in, gv_ref), (scaled.at[0], dres_ref), (scaled.at[1], drate_ref))
        )
    ]
    for copy in copies[:3]:
        copy.start()
    scaled[0] = dres_in[...] * scale_in[...]
    copies[3].start()
    scaled[1] = drate_in[...] * scale_in[...]
    copies[4].start()
    for copy in copies:
        copy.wait()


def per_device(n, ntp, grad_out, query_in, key_in, value_in, residue, log_rate):
    rows, chans = grad_out.shape
    modes = residue.shape[1]
    span = rows // SUB
    chunks = chans // LANES
    pairs = n // 2
    groups = GROUPS if chunks % (2 * GROUPS) == 0 and n <= 32 else 1
    width = chans // groups
    half = width // 2
    own = -(-(half // LANES * 2 * modes // SUB) // pairs)
    f32 = jnp.float32
    shape = jax.ShapeDtypeStruct
    hbm = pl.BlockSpec(memory_space=pltpu.HBM)
    vmem = pl.BlockSpec(memory_space=pltpu.VMEM)
    buffer = lambda *dims: pltpu.VMEM(dims, f32)
    tile = lambda *lead: pltpu.VMEM((*lead, SUB, LANES), f32)
    flags = lambda *dims: pltpu.SemaphoreType.DMA(dims)
    wide_out = pltpu.VMEM((rows, chans), grad_out.dtype)
    results = pl.pallas_call(
        functools.partial(fused_kernel, n, ntp, modes, groups),
        out_shape=(wide_out,) * 3 + (pltpu.VMEM((modes, chans), f32),) * 3,
        in_specs=[hbm] * 6,
        out_specs=(vmem,) * 6,
        scratch_shapes=[
            *[pltpu.VMEM((rows, chans), grad_out.dtype)] * 4,
            buffer(modes, chans),
            buffer(modes, chans),
            buffer(chunks, rows, LANES),
            buffer(chunks, rows, LANES),
            buffer(chunks, 2, modes * SUB, LANES),
            buffer(chunks, 2, SUB, modes, LANES),
            buffer(groups, 2, 4, modes, half),
            buffer(2, modes * SUB, LANES),
            buffer(2 * span * SUB, LANES),
            buffer(span, LANES),
            buffer((span + 1) * modes, LANES),
            buffer(rows, LANES),
            buffer(rows, LANES),
            buffer(groups, 2, 2, modes, half),
            buffer(groups, 2, modes, half),
            buffer(groups, 4, modes, half),
            buffer(groups, 2, modes, half),
            buffer(groups, pairs - 1, modes, half),
            buffer(groups, 2, 2, modes, half),
            buffer(groups, 2, modes, half),
            tile(groups, own * pairs),
            tile(groups, pairs - 1, own),
            tile(groups, own),
            tile(groups, 2, pairs, own),
            tile(),
            tile(2 * ntp),
            flags(4, groups), flags(2),
            flags(groups), flags(groups),
            flags(groups), flags(groups),
            flags(groups, pairs - 1), flags(groups, pairs - 1),
            flags(groups), flags(groups),
            flags(groups, pairs - 1), flags(groups, pairs - 1),
            flags(groups, pairs - 1), flags(groups, pairs - 1),
            flags(groups), flags(groups),
            flags(2 * ntp - 1), flags(2 * ntp - 1),
        ],
        compiler_params=pltpu.CompilerParams(
            collective_id=0, has_side_effects=True, vmem_limit_bytes=VMEM_BYTES
        ),
        name="fused",
    )(grad_out, query_in, key_in, value_in, log_rate.T, residue.T)
    anywhere = pl.BlockSpec(memory_space=pl.ANY)
    wide, tall = shape((rows, chans), grad_out.dtype), shape((modes, chans), f32)
    grad_query, grad_key, grad_value, d_res, d_rate = pl.pallas_call(
        settle_kernel,
        out_shape=(wide,) * 3 + (tall,) * 2,
        in_specs=[anywhere] * 3 + [vmem] * 3,
        out_specs=(anywhere,) * 5,
        scratch_shapes=[buffer(2, modes, chans), flags(5)],
        compiler_params=pltpu.CompilerParams(vmem_limit_bytes=SETTLE_BYTES),
        name="settle",
    )(*results)
    return grad_query, grad_key, grad_value, d_res.T, d_rate.T


def solution(mesh):
    wide = P("ctx", "tp")
    tall = P("tp", None)
    body = functools.partial(per_device, mesh.shape["ctx"], mesh.shape["tp"])
    return jax.shard_map(
        body,
        mesh=mesh,
        in_specs=(wide,) * 4 + (tall,) * 2,
        out_specs=(wide,) * 3 + (tall,) * 2,
        check_vma=False,
    )
```

```python
import functools

import jax
import jax.numpy as jnp
from jax import lax
from jax.experimental import pallas as pl
from jax.experimental.pallas import tpu as pltpu
from jax.sharding import PartitionSpec as P

CLIP_NORM = 512
SUB = 8
LANES = 128
MESH = pl.DeviceIdType.MESH
VMEM_BYTES = 56 * 1024 * 1024
SETTLE_BYTES = 4 * 1024 * 1024
GROUPS = 4
STARTS = (2, 3, 4, 4)
FINISHES = (7, 7, 8, 8)
PASSES = (11, 11, 11, 11)


def total_of(terms):
    while len(terms) > 1:
        paired = [x + y for x, y in zip(terms[::2], terms[1::2])]
        terms = paired + ([terms[-1]] if len(terms) % 2 else [])
    return terms[0]


def fused_kernel(
    n, ntp, modes, groups,
    go_in, q_in, k_in, v_in, lr_in, res_in,
    gq_ref, gk_ref, gv_ref, dres_ref, drate_ref, scale_ref,
    go_ref, q_ref, k_ref, v_ref, lr_ref, res_ref,
    p_s, g_s, ends_s, pre_s, loc_s, turn_s, lag_s, hold_s, table, fr_s, br_s,
    ea_s, mate, mate_loc, pt_s, held, ca_s, back_s, raw_s, parts, red, gath, sums, squares,
    in_sem, small_sem, pa_send, pa_recv, pl_send, pl_recv, ex_send, ex_recv, bk_send, bk_recv,
    rs_send, rs_recv, ag_send, ag_recv, fw_send, fw_recv, sq_send, sq_recv,
):
    me = lax.axis_index("ctx")
    col = lax.axis_index("tp")
    pair = me // 2
    odd = lax.rem(me, 2)
    pairs = n // 2
    plane = 2 * ntp
    here = odd * ntp + col
    rows, chans = go_ref.shape
    span = rows // SUB
    width = chans // groups
    half = width // 2
    chunks = chans // LANES
    per_group = width // LANES
    per_half = half // LANES
    pieces = 2 * modes // SUB
    own = red.shape[1]
    zero = jnp.zeros((SUB, LANES), jnp.float32)
    folds = modes // SUB

    def fetch(which, g):
        at = pl.ds(pl.multiple_of(g * width, LANES), width)
        source = (go_in, q_in, k_in, v_in)[which]
        target = (go_ref, q_ref, k_ref, v_ref)[which]
        return pltpu.make_async_copy(source.at[:, at], target.at[:, at], in_sem.at[which, g])

    rate_copy = pltpu.make_async_copy(lr_in, lr_ref, small_sem.at[0])
    residue_copy = pltpu.make_async_copy(res_in, res_ref, small_sem.at[1])
    rate_copy.start()
    for g in range(groups):
        for which in (2, 3, 0, 1):
            fetch(which, g).start()
    residue_copy.start()

    def beside(q):
        other = lax.rem(here + q, plane)
        return {"ctx": pair * 2 + other // ntp, "tp": lax.rem(other, ntp)}

    def along(k):
        return {"ctx": lax.rem(pair + k, pairs) * 2 + odd}

    across_pair = {"ctx": pair * 2 + 1 - odd}
    barrier = pltpu.get_barrier_semaphore()
    for q in range(1, plane):
        pl.semaphore_signal(barrier, inc=1, device_id=beside(q), device_id_type=MESH)
    for k in range(1, pairs):
        pl.semaphore_signal(barrier, inc=1, device_id=along(k), device_id_type=MESH)

    def wide(x, m):
        return jnp.broadcast_to(x[m : m + 1], (SUB, LANES))

    def lanes(ch):
        return pl.ds(pl.multiple_of(ch * LANES, LANES), LANES)

    def fold(f):
        return pl.ds(f * SUB, SUB)

    def turned(q, f):
        return pl.ds(f * SUB * SUB + q, SUB, stride=SUB)

    def copy_to(source, target, send, recv, place):
        return pltpu.make_async_remote_copy(
            src_ref=source, dst_ref=target, send_sem=send, recv_sem=recv, device_id=place, device_id_type=MESH
        )

    def ends(ch):
        g, c = ch // per_group, lax.rem(ch, per_group)
        at = lanes(ch)
        p_s[ch] = k_ref[:, at].astype(jnp.float32) * v_ref[:, at].astype(jnp.float32)
        g_s[ch] = go_ref[:, at].astype(jnp.float32) * q_ref[:, at].astype(jnp.float32)
        rate = jnp.exp(lr_ref[:, at])
        decay = jnp.exp(-rate)
        for first in range(0, modes, 8):
            group = range(first, min(modes, first + 8))
            a = [wide(decay, m) for m in group]
            s = [zero] * len(a)
            t = [zero] * len(a)
            for i in range(span):
                x = p_s[ch, pl.ds(i, SUB, stride=span), :]
                y = g_s[ch, pl.ds(span - 1 - i, SUB, stride=span), :]
                s = [aa * ss + x for aa, ss in zip(a, s)]
                t = [aa * tt + y for aa, tt in zip(a, t)]
            for slot, m in enumerate(group):
                ends_s[ch, 0, m * SUB : (m + 1) * SUB] = s[slot]
                ends_s[ch, 1, m * SUB : (m + 1) * SUB] = t[slot]
        far = jnp.exp(-rate * span)
        side, inner = c // per_half, lanes(lax.rem(c, per_half))
        for f in range(folds):
            step = far[f * SUB : (f + 1) * SUB]
            s = zero
            t = zero
            for q in range(SUB):
                pre_s[ch, 0, q, fold(f)] = s
                s = step * s + ends_s[ch, 0, turned(q, f)]
                pre_s[ch, 1, SUB - 1 - q, fold(f)] = t
                t = step * t + ends_s[ch, 1, turned(SUB - 1 - q, f)]
            ea_s[g, side, 0, fold(f), inner] = s
            ea_s[g, side, 1, fold(f), inner] = t

    def local(ch):
        g, c = ch // per_group, lax.rem(ch, per_group)
        side, inner = c // per_half, lanes(lax.rem(c, per_half))
        rate = jnp.exp(lr_ref[:, lanes(ch)])
        decay = jnp.exp(-rate)
        power = decay
        for k in range(1, span + 1):
            table[k * modes : (k + 1) * modes] = power * float(k)
            power = power * decay
        x = [p_s[ch, pl.ds(b, SUB, stride=span), :] for b in range(span)]
        y = [g_s[ch, pl.ds(b, SUB, stride=span), :] for b in range(span)]
        for m in range(modes):
            da, de = [], []
            for k in range(1, span + 1):
                coeff = jnp.broadcast_to(table[k * modes + m : k * modes + m + 1], (SUB, LANES))
                da.append(coeff * y[k - 1])
                if k < span:
                    de.append(coeff * x[span - 1 - k])
                if len(da) == 4:
                    da = [total_of(da)]
                if len(de) == 4:
                    de = [total_of(de)]
            turn_s[0, m * SUB : (m + 1) * SUB] = total_of(da)
            turn_s[1, m * SUB : (m + 1) * SUB] = total_of(de)
        for j in range(span):
            terms = []
            for b in range(span - j):
                terms.append(y[b + j] * x[b])
                if len(terms) == 4:
                    terms = [total_of(terms)]
            lag_s[j * SUB : (j + 1) * SUB] = total_of(terms)
        for f in range(span // SUB):
            hold_s[f * SUB : (f + 1) * SUB] = total_of([lag_s[turned(q, f)] for q in range(SUB)])
        far = jnp.exp(-rate * span)
        for f in range(folds):
            a = decay[f * SUB : (f + 1) * SUB]
            step = far[f * SUB : (f + 1) * SUB]
            v = zero
            d = zero
            for j in reversed(range(span)):
                d = a * d + v
                v = a * v + jnp.broadcast_to(hold_s[j : j + 1], (SUB, LANES))
            z = a * step * float(span)
            raw = zero
            lag = zero
            ahead = zero
            behind = zero
            for q in range(SUB):
                before = pre_s[ch, 0, q, fold(f)]
                after = pre_s[ch, 1, q, fold(f)]
                u = turn_s[0, turned(q, f)] + z * after
                w = a * turn_s[1, turned(q, f)]
                raw = raw + before * ends_s[ch, 1, turned(q, f)]
                lag = lag + before * u + after * w
                behind = step * behind + w + z * before
            for q in reversed(range(SUB)):
                u = turn_s[0, turned(q, f)] + z * pre_s[ch, 1, q, fold(f)]
                ahead = step * ahead + u
            loc_s[g, side, 0, fold(f), inner] = v + a * raw
            loc_s[g, side, 1, fold(f), inner] = a * d + lag
            loc_s[g, side, 2, fold(f), inner] = ahead
            loc_s[g, side, 3, fold(f), inner] = behind

    def couple(g):
        return copy_to(ea_s.at[g, 1 - odd], mate.at[g], pa_send.at[g], pa_recv.at[g], across_pair)

    def pool(g):
        return copy_to(loc_s.at[g, 1 - odd], mate_loc.at[g], pl_send.at[g], pl_recv.at[g], across_pair)

    def exchange(g, k):
        there = lax.rem(pair + k, pairs)
        which = jnp.where(there < pair, 1, 0)
        return copy_to(
            pt_s.at[g, which], held.at[g, k - 1], ex_send.at[g, k - 1], ex_recv.at[g, k - 1], along(k)
        )

    def hand(g):
        return copy_to(back_s.at[g], ca_s.at[g, odd], bk_send.at[g], bk_recv.at[g], across_pair)

    def scatter(g, k):
        there = lax.rem(pair + k, pairs)
        return copy_to(
            raw_s.at[g, pl.ds(there * own, own)],
            parts.at[g, k - 1], rs_send.at[g, k - 1], rs_recv.at[g, k - 1], along(k),
        )

    def gather(g, k):
        return copy_to(red.at[g], gath.at[g, odd, pair], ag_send.at[g, k - 1], ag_recv.at[g, k - 1], along(k))

    def forward(g):
        return copy_to(gath.at[g, odd], gath.at[g, odd], fw_send.at[g], fw_recv.at[g], across_pair)

    def norm(q):
        return copy_to(squares.at[here], squares.at[here], sq_send.at[q - 1], sq_recv.at[q - 1], beside(q))

    def rates(g):
        at = pl.ds(pl.multiple_of(g * width + odd * half, LANES), half)
        return jnp.exp(lr_ref[:, at])

    def ordered(g):
        mine, other = ea_s[g, odd], mate[g]
        return jnp.where(odd == 1, other, mine), jnp.where(odd == 1, mine, other)

    def join(g):
        couple(g).wait_recv()
        across = jnp.exp(-rates(g) * rows)
        early, late = ordered(g)
        pt_s[g, 0] = across * early[0] + late[0]
        pt_s[g, 1] = early[1] + across * late[1]
        for k in range(1, pairs):
            exchange(g, k).start()

    def carry(g):
        rate = rates(g)
        back_s[g] = jnp.zeros_like(back_s[g])
        for k in range(1, pairs):
            exchange(g, k).wait_recv()
            origin = lax.rem(pair - k + pairs, pairs)
            which = jnp.where(origin < pair, 0, 1)
            gap = jnp.where(origin < pair, pair - origin, origin - pair) - 1
            power = jnp.exp(-rate * (gap * (2 * rows)).astype(jnp.float32))
            back_s[g, which] += power * held[g, k - 1]
        across = jnp.exp(-rate * rows)
        early, late = ordered(g)
        from_past = back_s[g, 0]
        from_next = back_s[g, 1]
        past = from_past, early[0] + across * from_past
        ahead = late[1] + across * from_next, from_next
        ca_s[g, odd, 0] = jnp.where(odd == 1, past[1], past[0])
        ca_s[g, odd, 1] = jnp.where(odd == 1, ahead[1], ahead[0])
        back_s[g, 0] = jnp.where(odd == 1, past[0], past[1])
        back_s[g, 1] = jnp.where(odd == 1, ahead[0], ahead[1])
        hand(g).start()

    def grads(g, c):
        inner = lanes(c)
        at = pl.ds(pl.multiple_of(g * width + odd * half + c * LANES, LANES), LANES)
        rate = jnp.exp(lr_ref[:, at])
        decay = jnp.exp(-rate)
        root = jnp.sqrt(2.0 * rate)
        weight = res_ref[:, at] * root
        through = jnp.exp(-rate * (rows + 1)) * float(rows)
        raw, lag = [], []
        for loc, past, ahead, first in (
            (loc_s.at[g, odd], ca_s[g, odd, 0, :, inner], ca_s[g, odd, 1, :, inner], ea_s[g, odd, 1, :, inner]),
            (mate_loc.at[g], back_s[g, 0, :, inner], back_s[g, 1, :, inner], mate[g, 1, :, inner]),
        ):
            raw.append(loc[0, :, inner] + decay * (past * first))
            lag.append(
                loc[1, :, inner] + past * loc[2, :, inner] + ahead * (loc[3, :, inner] + through * past)
            )
        raw_weight = raw[0] + raw[1]
        both = (root * raw_weight, weight * (0.5 * raw_weight - rate * (lag[0] + lag[1])))
        for piece in range(pieces):
            low = piece % (pieces // 2) * SUB
            raw_s[g, c * pieces + piece] = both[piece // (pieces // 2)][low : low + SUB]

    def reduce_start(g):
        carry(g)
        pool(g).wait_recv()
        for c in range(per_half):
            grads(g, c)
        for k in range(1, pairs):
            scatter(g, k).start()

    def reduce_finish(g):
        mine = raw_s[g, pl.ds(pair * own, own)]
        for k in range(1, pairs):
            scatter(g, k).wait_recv()
            mine = mine + parts[g, k - 1]
        red[g] = mine
        for k in range(1, pairs):
            gather(g, k).start()
        gath[g, odd, pair] = mine

    def unpack(g, side):
        for c in range(per_half):
            at = pl.ds(pl.multiple_of(g * width + side * half + c * LANES, LANES), LANES)
            for piece in range(pieces):
                tile = c * pieces + piece
                low = piece % (pieces // 2) * SUB
                ref = dres_ref if piece < pieces // 2 else drate_ref
                ref[low : low + SUB, at] = gath[g, side, tile // own, tile % own]

    def pass_on(g):
        for k in range(1, pairs):
            gather(g, k).wait_recv()
        forward(g).start()
        whole = gath[g, odd]
        sums[...] += jnp.sum(jnp.sum(whole * whole, axis=0), axis=0)
        unpack(g, odd)

    def filters(ch):
        g, c = ch // per_group, lax.rem(ch, per_group)
        side, inner = c // per_half, lanes(lax.rem(c, per_half))
        at = lanes(ch)
        rate = jnp.exp(lr_ref[:, at])
        decay = jnp.exp(-rate)
        far = jnp.exp(-rate * span)
        for f in range(folds):
            step = far[f * SUB : (f + 1) * SUB]
            past = ca_s[g, side, 0, fold(f), inner]
            ahead = ca_s[g, side, 1, fold(f), inner]
            for q in range(SUB):
                turn_s[0, turned(q, f)] = pre_s[ch, 0, q, fold(f)] + past
                turn_s[1, turned(SUB - 1 - q, f)] = pre_s[ch, 1, SUB - 1 - q, fold(f)] + ahead
                past = step * past
                ahead = step * ahead
        power = res_ref[:, at] * jnp.sqrt(2.0 * rate)
        for k in range(span + 1):
            table[k * modes : (k + 1) * modes] = power
            power = power * decay
        for f in range(span // SUB):
            hold_s[f * SUB : (f + 1) * SUB] = total_of(
                [table[pl.ds(f * SUB * modes + m, SUB, stride=modes)] for m in range(modes)]
            )
        h = [jnp.broadcast_to(hold_s[j : j + 1], (SUB, LANES)) for j in range(span)]
        x = [p_s[ch, pl.ds(b, SUB, stride=span), :] for b in range(span)]
        for b in range(span):
            terms = []
            for j in range(b + 1):
                terms.append(h[j] * x[b - j])
                if len(terms) == 4:
                    terms = [total_of(terms)]
            lag_s[b * SUB : (b + 1) * SUB] = total_of(terms)
        y = [g_s[ch, pl.ds(b, SUB, stride=span), :] for b in range(span)]
        for b in range(span):
            terms = []
            for j in range(span - b):
                terms.append(h[j] * y[b + j])
                if len(terms) == 4:
                    terms = [total_of(terms)]
            lag_s[(span + b) * SUB : (span + b + 1) * SUB] = total_of(terms)
        s = [turn_s[0, m * SUB : (m + 1) * SUB] for m in range(modes)]
        t = [turn_s[1, m * SUB : (m + 1) * SUB] for m in range(modes)]
        for k in range(1, span + 1):
            b = k - 1
            r = span - k
            fore = [lag_s[b * SUB : (b + 1) * SUB]]
            back = [lag_s[(span + r) * SUB : (span + r + 1) * SUB]]
            for m in range(modes):
                coeff = jnp.broadcast_to(table[k * modes + m : k * modes + m + 1], (SUB, LANES))
                fore.append(coeff * s[m])
                back.append(coeff * t[m])
                if len(fore) == 4:
                    fore = [total_of(fore)]
                    back = [total_of(back)]
            fr_s[pl.ds(b, SUB, stride=span), :] = total_of(fore)
            br_s[pl.ds(r, SUB, stride=span), :] = total_of(back)
        gq_ref[:, at] = (go_ref[:, at].astype(jnp.float32) * fr_s[...]).astype(gq_ref.dtype)
        back = br_s[...]
        gk_ref[:, at] = (back * v_ref[:, at].astype(jnp.float32)).astype(gk_ref.dtype)
        gv_ref[:, at] = (back * k_ref[:, at].astype(jnp.float32)).astype(gv_ref.dtype)

    if raw_s.shape[1] > per_half * pieces:
        raw_s[...] = jnp.zeros_like(raw_s)

    def part(g, theirs, c):
        return g * per_group + jnp.where(theirs, 1 - odd, odd) * per_half + c

    def each(act, g, theirs):
        def one(c, _):
            act(part(g, theirs, c))
            return 0

        lax.fori_loop(0, per_half, one, 0)

    def first_stage(g, _):
        for which in range(4):
            fetch(which, g).wait()
        each(ends, g, True)

        @pl.when(g == 0)
        def _():
            pl.semaphore_wait(barrier, plane + pairs - 2)

        couple(g).start()
        return 0

    def second_stage(g, _):
        each(local, g, True)
        pool(g).start()
        each(ends, g, False)
        join(g)
        return 0

    def start_at(h):
        return STARTS[h] if groups == GROUPS else h

    def finish_at(h):
        return FINISHES[h] if groups == GROUPS else 3 * groups - 1

    def drain(g, _):
        couple(g).wait_send()
        pool(g).wait_send()
        hand(g).wait_send()
        for k in range(1, pairs):
            exchange(g, k).wait_send()
            scatter(g, k).wait_send()
            gather(g, k).wait_send()
        return 0

    def pass_at(h):
        return PASSES[h] if groups == GROUPS else 3 * groups - 1

    def third_stage(g, _):
        each(local, g, False)
        for h in range(groups):
            if start_at(h) < groups:
                pl.when(g == start_at(h))(functools.partial(reduce_start, h))
        return 0

    def fourth_stage(i, _):
        theirs = i // groups == 1
        g = lax.rem(i, groups)

        @pl.when(theirs)
        def _():
            hand(g).wait_recv()

        each(filters, g, theirs)
        for h in range(groups):
            if start_at(h) >= groups:
                pl.when(i == start_at(h) - groups)(functools.partial(reduce_start, h))
        for h in range(groups):
            pl.when(i == max(finish_at(h) - groups, 0))(functools.partial(reduce_finish, h))
        for h in range(groups):
            pl.when(i == pass_at(h) - groups)(functools.partial(pass_on, h))
        return 0

    sums[...] = zero
    rate_copy.wait()
    lax.fori_loop(0, groups, first_stage, 0)
    lax.fori_loop(0, groups, second_stage, 0)
    residue_copy.wait()
    lax.fori_loop(0, groups, third_stage, 0)
    lax.fori_loop(0, 2 * groups, fourth_stage, 0)
    squares[here] = sums[...]
    for q in range(1, plane):
        norm(q).start()
    lax.fori_loop(0, groups, drain, 0)
    for g in range(groups):
        forward(g).wait_recv()
        unpack(g, 1 - odd)
    for q in range(1, plane):
        norm(q).wait()
    square = jnp.sum(jnp.sum(squares[...], axis=0), keepdims=True)
    scale = jnp.minimum(1.0, CLIP_NORM / jnp.sqrt(square + 1e-06))
    scale_ref[...] = jnp.broadcast_to(scale, scale_ref.shape)
    for g in range(groups):
        forward(g).wait_send()


def settle_kernel(
    gq_in, gk_in, gv_in, dres_in, drate_in, scale_in,
    gq_ref, gk_ref, gv_ref, dres_ref, drate_ref, scaled, sem,
):
    copies = [
        pltpu.make_async_copy(source, target, sem.at[i])
        for i, (source, target) in enumerate(
            ((gq_in, gq_ref), (gk_in, gk_ref), (gv_in, gv_ref), (scaled.at[0], dres_ref), (scaled.at[1], drate_ref))
        )
    ]
    for copy in copies[:3]:
        copy.start()
    scaled[0] = dres_in[...] * scale_in[...]
    copies[3].start()
    scaled[1] = drate_in[...] * scale_in[...]
    copies[4].start()
    for copy in copies:
        copy.wait()


def per_device(n, ntp, grad_out, query_in, key_in, value_in, residue, log_rate):
    rows, chans = grad_out.shape
    modes = residue.shape[1]
    span = rows // SUB
    chunks = chans // LANES
    pairs = n // 2
    groups = GROUPS if chunks % (2 * GROUPS) == 0 and n <= 32 else 1
    width = chans // groups
    half = width // 2
    own = -(-(half // LANES * 2 * modes // SUB) // pairs)
    f32 = jnp.float32
    shape = jax.ShapeDtypeStruct
    hbm = pl.BlockSpec(memory_space=pltpu.HBM)
    vmem = pl.BlockSpec(memory_space=pltpu.VMEM)
    buffer = lambda *dims: pltpu.VMEM(dims, f32)
    tile = lambda *lead: pltpu.VMEM((*lead, SUB, LANES), f32)
    flags = lambda *dims: pltpu.SemaphoreType.DMA(dims)
    wide_out = pltpu.VMEM((rows, chans), grad_out.dtype)
    results = pl.pallas_call(
        functools.partial(fused_kernel, n, ntp, modes, groups),
        out_shape=(wide_out,) * 3 + (pltpu.VMEM((modes, chans), f32),) * 3,
        in_specs=[hbm] * 6,
        out_specs=(vmem,) * 6,
        scratch_shapes=[
            *[pltpu.VMEM((rows, chans), grad_out.dtype)] * 4,
            buffer(modes, chans),
            buffer(modes, chans),
            buffer(chunks, rows, LANES),
            buffer(chunks, rows, LANES),
            buffer(chunks, 2, modes * SUB, LANES),
            buffer(chunks, 2, SUB, modes, LANES),
            buffer(groups, 2, 4, modes, half),
            buffer(2, modes * SUB, LANES),
            buffer(2 * span * SUB, LANES),
            buffer(span, LANES),
            buffer((span + 1) * modes, LANES),
            buffer(rows, LANES),
            buffer(rows, LANES),
            buffer(groups, 2, 2, modes, half),
            buffer(groups, 2, modes, half),
            buffer(groups, 4, modes, half),
            buffer(groups, 2, modes, half),
            buffer(groups, pairs - 1, modes, half),
            buffer(groups, 2, 2, modes, half),
            buffer(groups, 2, modes, half),
            tile(groups, own * pairs),
            tile(groups, pairs - 1, own),
            tile(groups, own),
            tile(groups, 2, pairs, own),
            tile(),
            tile(2 * ntp),
            flags(4, groups), flags(2),
            flags(groups), flags(groups),
            flags(groups), flags(groups),
            flags(groups, pairs - 1), flags(groups, pairs - 1),
            flags(groups), flags(groups),
            flags(groups, pairs - 1), flags(groups, pairs - 1),
            flags(groups, pairs - 1), flags(groups, pairs - 1),
            flags(groups), flags(groups),
            flags(2 * ntp - 1), flags(2 * ntp - 1),
        ],
        compiler_params=pltpu.CompilerParams(
            collective_id=0, has_side_effects=True, vmem_limit_bytes=VMEM_BYTES
        ),
        name="fused",
    )(grad_out, query_in, key_in, value_in, log_rate.T, residue.T)
    anywhere = pl.BlockSpec(memory_space=pl.ANY)
    wide, tall = shape((rows, chans), grad_out.dtype), shape((modes, chans), f32)
    grad_query, grad_key, grad_value, d_res, d_rate = pl.pallas_call(
        settle_kernel,
        out_shape=(wide,) * 3 + (tall,) * 2,
        in_specs=[anywhere] * 3 + [vmem] * 3,
        out_specs=(anywhere,) * 5,
        scratch_shapes=[buffer(2, modes, chans), flags(5)],
        compiler_params=pltpu.CompilerParams(vmem_limit_bytes=SETTLE_BYTES),
        name="settle",
    )(*results)
    return grad_query, grad_key, grad_value, d_res.T, d_rate.T


def solution(mesh):
    wide = P("ctx", "tp")
    tall = P("tp", None)
    body = functools.partial(per_device, mesh.shape["ctx"], mesh.shape["tp"])
    return jax.shard_map(
        body,
        mesh=mesh,
        in_specs=(wide,) * 4 + (tall,) * 2,
        out_specs=(wide,) * 3 + (tall,) * 2,
        check_vma=False,
    )
```
